32 devices in a mesh: groups: 2 (over x), seq: 16 (over z, y, core).
Axes of the slice: x: 2, y: 2, z: 4, core: 2. Of those that a mesh axis runs over, the one named last changes fastest.
Arguments:
- video: bfloat16 [32, 256, 1152], P(('groups', 'seq')), parts along dimension 0, may hold values from -6 to 6
- spatial_qkv: bfloat16 [1152, 3456], P(None, 'seq'), may hold values from -0.53033009 to 0.53033009
- spatial_out: bfloat16 [1152, 1152], P(None, 'seq'), may hold values from -0.1875 to 0.1875
- temporal_qkv: bfloat16 [1152, 3456], P(None, 'seq'), may hold values from -0.53033009 to 0.53033009
- temporal_out: bfloat16 [1152, 1152], P(None, 'seq'), may hold values from -0.1875 to 0.1875
Outputs:
- video_out: bfloat16 [32, 256, 1152], P(('groups', 'seq')), parts along dimension 0
The draws below stay inside these ranges and needn't reach their ends.
There are 2 independent parts, one for each index of `groups`. The reference program is written for one: setup_inputs(seed, part) draws one part's arguments, and reference() takes and returns one part's arrays. A program takes and returns all parts, laid end to end along the dimension named above; an argument that names none is the same for every part. Nothing has to cross between parts.
All inputs are finite; a program needn't handle non-finite values.
Results may differ from the reference program's by a relative error of at most 0.023.
The reference program's roundings to bfloat16 on the way count: a program that leaves them out, or rounds other values in their place, can miss the bound.
Values may be sent and summed in bfloat16 or wider, within the bound.
A program may use at most 128 MiB of HBM per device.

```python
import math
import jax
import jax.numpy as jnp
from jax import lax

D = 1152
HEADS = 16
PATCHES = 256
FRAMES = 16


def qkv_table(key):
    deviation = D ** (-0.5)
    base = jax.random.truncated_normal(key, -4.0, 4.0, (D, 3 * D), jnp.float32) * deviation
    boost = 1.0
    column = lax.broadcasted_iota(jnp.int32, (1, 3 * D), 1)
    factor = jnp.where(column < 2 * D, boost, 1.0)
    return base * factor


def draw_spatial_qkv(key, part):
    return qkv_table(jax.random.fold_in(key, 11)).astype(jnp.bfloat16)


def draw_temporal_qkv(key, part):
    return qkv_table(jax.random.fold_in(key, 29)).astype(jnp.bfloat16)


def level_of(own_key, shape, shards, least, top_value):
    gain, own = 1.0, jax.random.fold_in(own_key, 6)
    for axis_at, blocks in shards:
        heights = jnp.exp(jax.random.uniform(jax.random.fold_in(own, axis_at), (blocks,), jnp.float32, least / len(shards), top_value / len(shards)))
        gain = gain * jnp.repeat(heights, shape[axis_at] // blocks).reshape([-1 if axis == axis_at else 1 for axis in range(len(shape))])
    return gain


def bell_draw(key, extent, scale, reach, shards=(), kind=jnp.bfloat16):
    values = jax.random.normal(key, extent, jnp.float32) * scale
    if len(shards) > 0:
        values = level_of(key, extent, shards, -0.22, 0.18) * values
    return jnp.clip(values, min=-reach, max=reach).astype(kind)


def setup_inputs(seed: int = 0, part: int = 0) -> dict:
    splits = jax.random.split(jax.random.key(seed), 6)
    own_keys = jax.random.split(jax.random.fold_in(splits[5], part), 6)
    return {
        "video": bell_draw(own_keys[0], (FRAMES, PATCHES, D), 1.0, 6.0, ((0, 16),)),
        "spatial_qkv": draw_spatial_qkv(jax.random.fold_in(splits[5], 71), part),
        "spatial_out": bell_draw(splits[2], (D, D), D ** -0.5, 0.1875, ((1, 16),)),
        "temporal_qkv": draw_temporal_qkv(jax.random.fold_in(splits[5], 71), part),
        "temporal_out": bell_draw(splits[4], (D, D), D ** -0.5, 0.1875, ((1, 16),)),
    }


epsilon = 1e-06

def normalize(values):
    average = lax.optimization_barrier(jnp.mean(values, axis=-1, keepdims=True))
    centered = values - average
    spread = lax.optimization_barrier(jnp.mean(centered * centered, axis=-1, keepdims=True))
    return (centered * lax.rsqrt(spread + epsilon)).astype(jnp.bfloat16)

def split_heads(table, leading, second, which):
    width = table.shape[1] // 3
    block = table[:, which * width:(which + 1) * width]
    return block.reshape(leading, second, HEADS, width // HEADS)

def attend(queries, key_rows, value_rows, score_form, mix_form):
    head_width = queries.shape[-1]

    def one_head(parts):
        head_query, head_key, head_value = parts
        scores = jnp.einsum(score_form, head_query.astype(jnp.float32), head_key.astype(jnp.float32)) / math.sqrt(head_width)
        highest = lax.optimization_barrier(jnp.max(scores, axis=-1, keepdims=True))
        powers = jnp.exp(scores - highest)
        probs = (powers / lax.optimization_barrier(jnp.sum(powers, axis=-1, keepdims=True))).astype(jnp.bfloat16)
        return jnp.einsum(mix_form, probs.astype(jnp.float32), head_value.astype(jnp.float32)).astype(jnp.bfloat16)
    stacked = lax.map(one_head, (jnp.moveaxis(queries, 2, 0), jnp.moveaxis(key_rows, 2, 0), jnp.moveaxis(value_rows, 2, 0)))
    moved = jnp.moveaxis(stacked, 0, 2)
    return moved.reshape(moved.shape[0], moved.shape[1], -1)

def sublayer(tokens, qkv_weight, out_weight, score_form, mix_form):
    frames, patches, width = tokens.shape
    rows = tokens.reshape(frames * patches, width)
    normed = normalize(rows.astype(jnp.float32))
    table = jnp.dot(normed, qkv_weight, preferred_element_type=jnp.float32).astype(jnp.bfloat16)
    mixed = attend(split_heads(table, frames, patches, 0), split_heads(table, frames, patches, 1), split_heads(table, frames, patches, 2), score_form, mix_form)
    update = jnp.dot(mixed.reshape(frames * patches, width), out_weight, preferred_element_type=jnp.float32)
    return (rows.astype(jnp.float32) + update).astype(jnp.bfloat16).reshape(frames, patches, width)

def reference(video, spatial_qkv, spatial_out, temporal_qkv, temporal_out):
    hidden = sublayer(video, spatial_qkv, spatial_out, 'fpe,fqe->fpq', 'fpq,fqe->fpe')
    return sublayer(hidden, temporal_qkv, temporal_out, 'fpe,gpe->pfg', 'pfg,gpe->fpe')
```

```python
import functools
import math

import jax
import jax.numpy as jnp
from jax import lax
from jax.experimental import pallas as pl
from jax.experimental.pallas import tpu as pltpu
from jax.sharding import PartitionSpec as P

HEADS = 16
epsilon = 1e-06
MESH = pl.DeviceIdType.MESH


def normalize_into(x_ref, xt_ref, nt_ref):
    xt_ref[...] = x_ref[...].astype(jnp.float32).T
    values = xt_ref[...]
    centered = values - jnp.mean(values, axis=0, keepdims=True)
    spread = jnp.mean(centered * centered, axis=0, keepdims=True)
    nt_ref[...] = (centered * lax.rsqrt(spread + epsilon)).astype(jnp.bfloat16)


def project_shard(w_ref, shard, nt_ref, table_ref):
    blocks, rows, width = w_ref.shape[1:]
    head = table_ref.shape[1]
    out = jnp.dot(
        w_ref[shard].reshape(blocks * rows, width), nt_ref[...], preferred_element_type=jnp.float32
    ).astype(jnp.bfloat16)
    for j in range(blocks):
        table_ref[shard * blocks + j] = out[j * rows : j * rows + head]


def attend_pair(pair, table_ref, mixed_ref, same, low=0, high=None):
    head = table_ref.shape[1]
    parts = []
    for j in range(2):
        h = pair * 2 + j
        q, k, v = table_ref[h, :, low:high], table_ref[HEADS + h], table_ref[2 * HEADS + h]
        scores = lax.dot_general(
            k, q, (((0,), (0,)), ((), ())), preferred_element_type=jnp.float32
        ) * (1.0 / math.sqrt(head))
        if same is not None:
            scores = jnp.where(same(scores.shape), scores, -jnp.inf)
        powers = jnp.exp(scores - jnp.max(scores, axis=0, keepdims=True))
        total = jnp.sum(powers, axis=0, keepdims=True)
        probs = (powers * (1.0 / total)).astype(jnp.bfloat16)
        parts.append(jnp.dot(v, probs, preferred_element_type=jnp.float32))
    both = jnp.concatenate(parts, axis=0).astype(jnp.bfloat16)
    mixed_ref[pl.ds(pl.multiple_of(pair * 2 * head, 16), 2 * head), low:high] = both


def project_out(w_ref, mixed_ref, xt_ref, out_ref, head, first=0, last=None):
    shards, blocks, rows, width = w_ref.shape
    low = head // 16 * 16
    step = 4
    tokens = slice(first, last)

    @pl.loop(0, shards // step)
    def _(i):
        weights = w_ref[pl.ds(i * step, step), :, low:, :].reshape(-1, width)
        update = jnp.dot(weights, mixed_ref[:, tokens], preferred_element_type=jnp.float32)
        update = update.reshape(step * blocks, rows - low, -1)[:, head - low :]
        count = step * blocks * (rows - head)
        at = pl.ds(pl.multiple_of(i * count, 8), count)
        xt_ref[at, tokens] = xt_ref[at, tokens] + update.reshape(count, -1)

    out_ref[tokens, :] = xt_ref[:, tokens].T.astype(jnp.bfloat16)


def same_by(kind, size):
    def same(shape):
        a = lax.broadcasted_iota(jnp.int32, shape, 0)
        b = lax.broadcasted_iota(jnp.int32, shape, 1)
        return (a % size == b % size) if kind == "mod" else (a // size == b // size)

    return same


def sublayer_kernel(same, x_ref, w_ref, out_ref, xt_ref, nt_ref, table_ref, mixed_ref):
    normalize_into(x_ref, xt_ref, nt_ref)

    @pl.loop(0, w_ref.shape[0])
    def _(d):
        project_shard(w_ref, d, nt_ref, table_ref)

    @pl.loop(0, HEADS // 2)
    def _(pair):
        attend_pair(pair, table_ref, mixed_ref, same)

    project_out(w_ref, mixed_ref, xt_ref, out_ref, table_ref.shape[1])


def compute_scratch(tokens, width):
    return [
        pltpu.VMEM((width, tokens), jnp.float32),
        pltpu.VMEM((width, tokens), jnp.bfloat16),
        pltpu.VMEM((3 * HEADS, width // HEADS, tokens), jnp.bfloat16),
        pltpu.VMEM((width, tokens), jnp.bfloat16),
    ]


def sublayer(x, w, same):
    tokens, width = x.shape
    return pl.pallas_call(
        functools.partial(sublayer_kernel, same),
        out_shape=jax.ShapeDtypeStruct(x.shape, jnp.bfloat16),
        in_specs=[pl.BlockSpec(memory_space=pltpu.VMEM)] * 2,
        out_specs=pl.BlockSpec(memory_space=pltpu.VMEM),
        scratch_shapes=compute_scratch(tokens, width),
        compiler_params=pltpu.CompilerParams(vmem_limit_bytes=40 << 20),
    )(x, w)


def blocks_of(qkv, out, count):
    width = qkv.shape[0]
    return jnp.concatenate(
        [qkv.T.reshape(count, -1, width), out.T.reshape(count, -1, width)], axis=1
    )


def gathered(qkv, out):
    if lax.axis_size("seq") == HEADS:
        return lax.all_gather(blocks_of(qkv, out, 3), "seq", axis=0)
    full = blocks_of(
        lax.all_gather(qkv, "seq", axis=1, tiled=True),
        lax.all_gather(out, "seq", axis=1, tiled=True),
        3 * HEADS,
    )
    return full.reshape(HEADS, 3, *full.shape[1:])


def plain(video, spatial_qkv, spatial_out, temporal_qkv, temporal_out):
    frames_here, patches, width = video.shape
    n = lax.axis_size("seq")
    count = patches // n
    same_s = None if frames_here == 1 else same_by("div", patches)
    hidden = sublayer(video.reshape(-1, width), gathered(spatial_qkv, spatial_out), same_s)
    blocks = hidden.reshape(frames_here, n, count, width)
    received = lax.all_to_all(blocks, "seq", split_axis=1, concat_axis=0, tiled=True)
    result = sublayer(
        received.reshape(-1, width), gathered(temporal_qkv, temporal_out), same_by("mod", count)
    )
    positioned = result.reshape(frames_here * n, 1, count, width)
    returned = lax.all_to_all(positioned, "seq", split_axis=0, concat_axis=1, tiled=True)
    return returned.reshape(frames_here, patches, width)


RANKS = 4


def pair_of(value, j):
    if j == 0:
        return value
    if j == 1:
        return value + 1 - 2 * lax.rem(value, 2)
    if j == 2:
        return lax.rem(value + 2, 4)
    return 3 - value


def attended(i, at, table_ref, same):
    heads = table_ref.shape[0] // 3
    head = table_ref.shape[2]
    q, k, v = table_ref[i, at], table_ref[heads + i, at], table_ref[2 * heads + i, at]
    scores = lax.dot_general(
        k, q, (((0,), (0,)), ((), ())), preferred_element_type=jnp.float32
    ) * (1.0 / math.sqrt(head))
    if same is not None:
        scores = jnp.where(same(scores.shape), scores, -jnp.inf)
    powers = jnp.exp(scores - jnp.max(scores, axis=0, keepdims=True))
    total = jnp.sum(powers, axis=0, keepdims=True)
    probs = (powers * (1.0 / total)).astype(jnp.bfloat16)
    return jnp.dot(v, probs, preferred_element_type=jnp.float32)


def fused_kernel(
    count, x_ref, sq_ref, so_ref, tq_ref, to_ref, out_ref,
    w_ref, na_ref, xt_ref, table_ref, ms_ref, mix_ref, nb_ref, g_ref, mt_ref, rs_ref, mr_ref,
    land_sem, deal_sem, line_sem, twin_sem, osib_sem, oy_sem, ox_sem, nland_sem, nsend_sem,
    msend_sem, mland_sem, asend_sem, gz_sem, fsend_sem, gr_sem, rsend_sem, rland_sem,
):
    n = HEADS
    me = lax.axis_index("seq")
    group = lax.axis_index("groups")
    z, r = lax.div(me, RANKS), lax.rem(me, RANKS)
    core, row = lax.rem(r, 2), lax.div(r, 2)
    side = lax.rem(group, 2)
    other = {"groups": group + 1 - 2 * side}
    sib = {"seq": RANKS * z + pair_of(r, 1)}
    far = {"seq": RANKS * z + pair_of(r, 2)}
    head = table_ref.shape[2]
    width, tokens = xt_ref.shape
    wide = RANKS * head

    def move(src, dst, send, recv, device):
        return pltpu.make_async_remote_copy(
            src_ref=src, dst_ref=dst, send_sem=send, recv_sem=recv,
            device_id=device, device_id_type=MESH,
        )

    sends = []

    def go(*what):
        one = move(*what)
        one.start()
        sends.append(one)


    def slot_of(pair, b):
        first = lax.rem(b + row, 2)
        second = 2 + (1 + r) * ((1 - row) * (1 - b) + row * b)
        return (1 - pair) * first + pair * second

    def mine(zz, b):
        return slot_of(lax.rem(zz + side, 2), b)

    def theirs(zz, b):
        return slot_of(1 - lax.rem(zz + side, 2), b)

    def block(phase, zz, slot, send, device):
        at = w_ref.at[phase, zz, slot]
        return move(at, at, send, land_sem.at[phase, zz, slot], device)

    def landed(phase, zz, slot):
        block(phase, zz, slot, deal_sem.at[0, 0], other).wait_recv()

    def line(phase, zz, b, way):
        device = {"seq": me + RANKS * (1 - 2 * way)}
        return block(phase, zz, mine(zz, b), line_sem.at[phase, way, zz, b], device)

    def twin(phase, zz, b):
        return block(phase, zz, mine(zz, b), twin_sem.at[phase, zz, b], other)

    def keep(phase, q_ref, o_ref):
        w_ref[phase, z, lax.div(3 * r + 2 * core, RANKS)] = q_ref[2 * core]
        w_ref[phase, z, 3 + r] = o_ref[0]

    def deal(phase, q_ref):
        for which, j, device in ((0, 2 - 2 * core, far), (1, 1, sib)):
            slot = lax.div(3 * r + j, RANKS)
            go(
                q_ref.at[j], w_ref.at[phase, z, slot], deal_sem.at[phase, which],
                land_sem.at[phase, z, slot], device,
            )

    def along(phase, b):
        j, source = (1, pair_of(r, 1)) if b == 0 else (2 - 2 * core, pair_of(r, 2))
        landed(phase, z, lax.div(3 * source + j, RANKS))

        @pl.when(z < RANKS - 1)
        def _():
            line(phase, z, b, 0).start()

        @pl.when(z > 0)
        def _():
            line(phase, z, b, 1).start()

    def hop(phase, d, b):
        @pl.when(z >= d)
        def _():
            landed(phase, z - d, mine(z - d, b))

            @pl.when(z < RANKS - 1)
            def _():
                line(phase, z - d, b, 0).start()

            twin(phase, z - d, b).start()

        @pl.when(z + d < RANKS)
        def _():
            landed(phase, z + d, mine(z + d, b))

            @pl.when(z > 0)
            def _():
                line(phase, z + d, b, 1).start()

            twin(phase, z + d, b).start()

    def from_twin(phase, zz):
        for b in range(2):
            landed(phase, zz, theirs(zz, b))

    def out_first(phase):
        for k in range(2):
            zz = 2 * k + 1 - side
            slot = 3 + r
            one = block(phase, zz, slot, oy_sem.at[phase, k], far)
            one.start()
            sends.append(one)
        for zz in range(RANKS):
            one = block(phase, zz, 3 + r, osib_sem.at[phase, zz, 0], sib)
            one.start()
            sends.append(one)

    def out_second(phase):
        slot = 3 + pair_of(r, 2)
        for k in range(2):
            zz = 2 * k + 1 - side
            landed(phase, zz, slot)
            for one in (
                block(phase, zz, slot, ox_sem.at[phase, k], other),
                block(phase, zz, slot, osib_sem.at[phase, zz, 1], sib),
            ):
                one.start()
                sends.append(one)

    def out_third(phase):
        slot = 3 + pair_of(r, 2)
        for k in range(2):
            zz = 2 * k + side
            landed(phase, zz, slot)
            one = block(phase, zz, slot, osib_sem.at[phase, zz, 1], sib)
            one.start()
            sends.append(one)

    def out_last(phase):
        for zz in range(RANKS):
            landed(phase, zz, 3 + pair_of(r, 1))
            landed(phase, zz, 3 + pair_of(r, 3))


    def normed(f, which, device):
        at = na_ref.at[f]
        return move(at, at, nsend_sem.at[which], nland_sem.at[f], device)

    def share(f, which, device):
        one = normed(f, which, device)
        one.start()
        sends.append(one)

    def project(zz, *frames):
        for f in frames:
            out = jnp.dot(
                w_ref[0, zz, 0:3].reshape(3 * head, width), na_ref[f],
                preferred_element_type=jnp.float32,
            )
            for slot in range(3):
                piece = out[slot * head : (slot + 1) * head]
                table_ref[3 * zz + slot, f] = piece.astype(jnp.bfloat16)

    def project_all(zz):
        @pl.loop(0, RANKS)
        def _(f):
            project(zz, f)

    def spatial_head(i):
        @pl.loop(0, 2)
        def _(t):
            for f in (2 * t, 2 * t + 1):
                ms_ref[i, f] = attended(i, f, table_ref, None).astype(jnp.bfloat16)

        for j in (2, 3, 1):
            f = pair_of(r, j)
            go(
                ms_ref.at[i, f], mix_ref.at[RANKS * i + r], msend_sem.at[i, j],
                mland_sem.at[RANKS * i + r], {"seq": RANKS * z + f},
            )
        mix_ref[RANKS * i + r] = ms_ref[i, r]

    def mixed():
        for j in range(1, RANKS):
            for i in range(RANKS):
                h = RANKS * i + pair_of(r, j)
                move(
                    ms_ref.at[0, 0], mix_ref.at[h], msend_sem.at[0, 1], mland_sem.at[h], other
                ).wait_recv()

    def project_back(phase):
        @pl.loop(0, RANKS)
        def _(zz):
            update = jnp.dot(
                w_ref[phase, zz, 3:7].reshape(wide, width), mix_ref[...].reshape(width, tokens),
                preferred_element_type=jnp.float32,
            )
            at = pl.ds(pl.multiple_of(zz * wide, 8), wide)
            xt_ref[at, :] = xt_ref[at, :] + update

    def normalize_again():
        values = xt_ref[...].astype(jnp.bfloat16).astype(jnp.float32)
        xt_ref[...] = values
        centered = values - jnp.mean(values, axis=0, keepdims=True)
        spread = jnp.mean(centered * centered, axis=0, keepdims=True)
        nb_ref[...] = (centered * lax.rsqrt(spread + epsilon)).T.astype(jnp.bfloat16)


    def rows(zz, part):
        return pl.ds(pl.multiple_of((RANKS * zz + part) * count, count), count)

    def scatter():
        for part in range(RANKS):
            for j in range(1, RANKS):
                to = pair_of(z, j)
                go(
                    nb_ref.at[rows(to, part)], g_ref.at[part, RANKS * r + z],
                    asend_sem.at[part, j], gz_sem.at[part, z], {"seq": RANKS * to + r},
                )
        for part in range(RANKS):
            g_ref[part, RANKS * r + z] = nb_ref[rows(z, part), :]

    def frames(part, rank, which, device):
        at = g_ref.at[part, pl.ds(RANKS * rank, RANKS)]
        return move(at, at, fsend_sem.at[part, which], gr_sem.at[part, rank], device)

    def forward(part):
        for j in range(1, RANKS):
            source = pair_of(z, j)
            move(
                nb_ref.at[rows(0, 0)], g_ref.at[part, RANKS * r + source],
                asend_sem.at[0, 1], gz_sem.at[part, source], other,
            ).wait_recv()
        frames(part, r, 1, far).start()
        frames(part, r, 0, sib).start()

    def relay(part):
        rank = pair_of(r, 2)
        frames(part, rank, 0, sib).wait_recv()
        frames(part, rank, 2, sib).start()

    def ready(part):
        for j in (1, 3):
            frames(part, pair_of(r, j), 0, sib).wait_recv()

    def temporal(part):
        out = lax.dot_general(
            w_ref[1, :, 0:3].reshape(3 * wide, width), g_ref[part].reshape(tokens, width),
            (((1,), (1,)), ((), ())), preferred_element_type=jnp.float32,
        )
        for slot in range(3 * RANKS):
            piece = out[slot * head : (slot + 1) * head]
            table_ref[slot, part] = piece.astype(jnp.bfloat16)

    def temporal_heads(part):
        @pl.loop(0, 2)
        def _(t):
            for i in (2 * t, 2 * t + 1):
                at = pl.ds(pl.multiple_of(i * head, 8), head)
                mt_ref[at, :] = attended(i, part, table_ref, same_by("mod", count))

        rs_ref[part] = mt_ref[...].T.astype(jnp.bfloat16).reshape(rs_ref.shape[1:])

    def back(part, j):
        to = lax.rem(me + j, n)
        zt, rt = lax.div(to, RANKS), lax.rem(to, RANKS)
        return move(
            rs_ref.at[part, RANKS * rt + zt], mr_ref.at[r, RANKS * z + part],
            rsend_sem.at[part, j], rland_sem.at[r, RANKS * z + part], {"seq": to},
        )

    def returned():
        for j in range(1, n):
            source = lax.rem(me + j, n)
            zt, rt = lax.div(source, RANKS), lax.rem(source, RANKS)
            for part in range(RANKS):
                move(
                    rs_ref.at[0, 0], mr_ref.at[rt, RANKS * zt + part],
                    rsend_sem.at[0, 1], rland_sem.at[rt, RANKS * zt + part], other,
                ).wait_recv()
        for rank in range(RANKS):
            turned = mr_ref[rank].reshape(tokens, -1).astype(jnp.float32).T
            for i in range(RANKS):
                piece = turned[i * head : (i + 1) * head]
                mix_ref[RANKS * i + rank] = piece.astype(jnp.bfloat16)

    barrier = pltpu.get_barrier_semaphore()
    for j in range(1, n):
        pl.semaphore_signal(
            barrier, inc=1, device_id={"seq": lax.rem(me + j, n)}, device_id_type=MESH
        )
    pl.semaphore_signal(barrier, inc=1, device_id=other, device_id_type=MESH)
    keep(0, sq_ref, so_ref)
    keep(1, tq_ref, to_ref)
    normalize_into(x_ref, xt_ref, na_ref.at[r])
    mt_ref[...] = jnp.zeros_like(mt_ref)
    pl.semaphore_wait(barrier, n)

    deal(0, sq_ref)
    along(0, 0)
    share(r, 1, far)
    share(r, 0, sib)
    along(0, 1)
    deal(1, tq_ref)
    hop(0, 1, 0)
    normed(pair_of(r, 1), 0, sib).wait_recv()
    project(z, r, pair_of(r, 1))
    hop(0, 1, 1)
    hop(0, 2, 0)
    normed(pair_of(r, 2), 0, sib).wait_recv()
    share(pair_of(r, 2), 2, sib)
    normed(pair_of(r, 3), 0, sib).wait_recv()
    project(z, pair_of(r, 2), pair_of(r, 3))
    from_twin(0, pair_of(z, 1))
    project_all(pair_of(z, 1))
    hop(0, 2, 1)
    along(1, 0)
    along(1, 1)
    hop(0, 3, 0)
    from_twin(0, pair_of(z, 2))
    project_all(pair_of(z, 2))
    hop(0, 3, 1)
    from_twin(0, pair_of(z, 3))
    project_all(pair_of(z, 3))
    out_first(0)
    hop(1, 1, 0)
    spatial_head(0)
    out_second(0)
    hop(1, 1, 1)
    spatial_head(1)
    out_third(0)
    hop(1, 2, 0)
    spatial_head(2)
    hop(1, 2, 1)
    spatial_head(3)
    hop(1, 3, 0)
    mixed()
    out_last(0)
    project_back(0)
    normalize_again()
    scatter()
    hop(1, 3, 1)
    forward(0)
    for j in range(1, RANKS):
        from_twin(1, pair_of(z, j))
    out_first(1)
    relay(0)
    out_second(1)

    @pl.loop(0, RANKS)
    def _(part):
        ready(part)

        @pl.when(part < RANKS - 1)
        def _():
            forward(part + 1)

        temporal(part)

        @pl.when(part < RANKS - 1)
        def _():
            relay(part + 1)

        temporal_heads(part)
        for j in range(1, n):
            back(part, j).start()
        mr_ref[r, RANKS * z + part] = rs_ref[part, RANKS * r + z]

    out_third(1)
    out_last(1)
    returned()
    project_back(1)
    out_ref[...] = xt_ref[...].T.astype(jnp.bfloat16)

    for one in sends:
        one.wait_send()
    for phase in range(2):
        for b in range(2):
            for zz in range(RANKS):

                @pl.when((z >= zz) & (z < RANKS - 1))
                def _():
                    line(phase, zz, b, 0).wait_send()

                @pl.when((z <= zz) & (z > 0))
                def _():
                    line(phase, zz, b, 1).wait_send()

            for j in range(1, RANKS):
                twin(phase, pair_of(z, j), b).wait_send()

    @pl.loop(0, RANKS)
    def _(part):
        for which, rank in ((0, r), (1, r), (2, pair_of(r, 2))):
            frames(part, rank, which, sib).wait_send()
        for j in range(1, n):
            back(part, j).wait_send()


def fused(video, spatial_qkv, spatial_out, temporal_qkv, temporal_out):
    _, tokens, width = video.shape
    n = lax.axis_size("seq")
    head, count = width // HEADS, tokens // n
    padded = -(-RANKS * head // 128) * 128
    vmem, dma = pltpu.VMEM, pltpu.SemaphoreType.DMA
    half = jnp.bfloat16

    def blocks(w):
        return w.T.reshape(-1, head, width)

    out = pl.pallas_call(
        functools.partial(fused_kernel, count),
        out_shape=jax.ShapeDtypeStruct((tokens, width), half),
        in_specs=[pl.BlockSpec(memory_space=pltpu.VMEM)] * 5,
        out_specs=pl.BlockSpec(memory_space=pltpu.VMEM),
        scratch_shapes=[
            vmem((2, RANKS, 3 + RANKS, head, width), half),
            vmem((RANKS, width, tokens), half),
            vmem((width, tokens), jnp.float32),
            vmem((3 * RANKS, RANKS, head, tokens), half),
            vmem((RANKS, RANKS, head, tokens), half),
            vmem((HEADS, head, tokens), half),
            vmem((tokens, width), half),
            vmem((RANKS, n, count, width), half),
            vmem((padded, tokens), jnp.float32),
            vmem((RANKS, n, count, padded), half),
            vmem((RANKS, n, count, padded), half),
            dma((2, RANKS, 3 + RANKS)),
            dma((2, 2)),
            dma((2, 2, RANKS, 2)),
            dma((2, RANKS, 2)),
            dma((2, RANKS, 2)),
            dma((2, 2)),
            dma((2, 2)),
            dma((RANKS,)),
            dma((3,)),
            dma((RANKS, RANKS)),
            dma((HEADS,)),
            dma((RANKS, RANKS)),
            dma((RANKS, RANKS)),
            dma((RANKS, 3)),
            dma((RANKS, RANKS)),
            dma((RANKS, n)),
            dma((RANKS, n)),
        ],
        compiler_params=pltpu.CompilerParams(
            collective_id=0, has_side_effects=True, vmem_limit_bytes=48 << 20
        ),
    )(
        video.reshape(tokens, width),
        blocks(spatial_qkv), blocks(spatial_out), blocks(temporal_qkv), blocks(temporal_out),
    )
    return out.reshape(video.shape)


def local(video, spatial_qkv, *rest):
    n, groups = lax.axis_size("seq"), lax.axis_size("groups")
    frames_here, patches, _ = video.shape
    ringed = n == HEADS and groups % 2 == 0 and frames_here == 1 and patches % (16 * n) == 0
    return (fused if ringed else plain)(video, spatial_qkv, *rest)


def solution(mesh):
    split = P(None, "seq")
    placed = (P(("groups", "seq"), None, None), split, split, split, split)
    return jax.shard_map(
        local,
        mesh=mesh,
        in_specs=placed,
        out_specs=placed[0],
        check_vma=False,
    )
```

```python
import functools
import math

import jax
import jax.numpy as jnp
from jax import lax
from jax.experimental import pallas as pl
from jax.experimental.pallas import tpu as pltpu
from jax.sharding import PartitionSpec as P

HEADS = 16
epsilon = 1e-06
MESH = pl.DeviceIdType.MESH


def normalize_into(x_ref, xt_ref, nt_ref):
    xt_ref[...] = x_ref[...].astype(jnp.float32).T
    values = xt_ref[...]
    centered = values - jnp.mean(values, axis=0, keepdims=True)
    spread = jnp.mean(centered * centered, axis=0, keepdims=True)
    nt_ref[...] = (centered * lax.rsqrt(spread + epsilon)).astype(jnp.bfloat16)


def project_shard(w_ref, shard, nt_ref, table_ref):
    blocks, rows, width = w_ref.shape[1:]
    head = table_ref.shape[1]
    out = jnp.dot(
        w_ref[shard].reshape(blocks * rows, width), nt_ref[...], preferred_element_type=jnp.float32
    ).astype(jnp.bfloat16)
    for j in range(blocks):
        table_ref[shard * blocks + j] = out[j * rows : j * rows + head]


def attend_pair(pair, table_ref, mixed_ref, same, low=0, high=None):
    head = table_ref.shape[1]
    parts = []
    for j in range(2):
        h = pair * 2 + j
        q, k, v = table_ref[h, :, low:high], table_ref[HEADS + h], table_ref[2 * HEADS + h]
        scores = lax.dot_general(
            k, q, (((0,), (0,)), ((), ())), preferred_element_type=jnp.float32
        ) * (1.0 / math.sqrt(head))
        if same is not None:
            scores = jnp.where(same(scores.shape), scores, -jnp.inf)
        powers = jnp.exp(scores - jnp.max(scores, axis=0, keepdims=True))
        total = jnp.sum(powers, axis=0, keepdims=True)
        probs = (powers * (1.0 / total)).astype(jnp.bfloat16)
        parts.append(jnp.dot(v, probs, preferred_element_type=jnp.float32))
    both = jnp.concatenate(parts, axis=0).astype(jnp.bfloat16)
    mixed_ref[pl.ds(pl.multiple_of(pair * 2 * head, 16), 2 * head), low:high] = both


def project_out(w_ref, mixed_ref, xt_ref, out_ref, head, first=0, last=None):
    shards, blocks, rows, width = w_ref.shape
    low = head // 16 * 16
    step = 4
    tokens = slice(first, last)

    @pl.loop(0, shards // step)
    def _(i):
        weights = w_ref[pl.ds(i * step, step), :, low:, :].reshape(-1, width)
        update = jnp.dot(weights, mixed_ref[:, tokens], preferred_element_type=jnp.float32)
        update = update.reshape(step * blocks, rows - low, -1)[:, head - low :]
        count = step * blocks * (rows - head)
        at = pl.ds(pl.multiple_of(i * count, 8), count)
        xt_ref[at, tokens] = xt_ref[at, tokens] + update.reshape(count, -1)

    out_ref[tokens, :] = xt_ref[:, tokens].T.astype(jnp.bfloat16)


def same_by(kind, size):
    def same(shape):
        a = lax.broadcasted_iota(jnp.int32, shape, 0)
        b = lax.broadcasted_iota(jnp.int32, shape, 1)
        return (a % size == b % size) if kind == "mod" else (a // size == b // size)

    return same


def sublayer_kernel(same, x_ref, w_ref, out_ref, xt_ref, nt_ref, table_ref, mixed_ref):
    normalize_into(x_ref, xt_ref, nt_ref)

    @pl.loop(0, w_ref.shape[0])
    def _(d):
        project_shard(w_ref, d, nt_ref, table_ref)

    @pl.loop(0, HEADS // 2)
    def _(pair):
        attend_pair(pair, table_ref, mixed_ref, same)

    project_out(w_ref, mixed_ref, xt_ref, out_ref, table_ref.shape[1])


def compute_scratch(tokens, width):
    return [
        pltpu.VMEM((width, tokens), jnp.float32),
        pltpu.VMEM((width, tokens), jnp.bfloat16),
        pltpu.VMEM((3 * HEADS, width // HEADS, tokens), jnp.bfloat16),
        pltpu.VMEM((width, tokens), jnp.bfloat16),
    ]


def sublayer(x, w, same):
    tokens, width = x.shape
    return pl.pallas_call(
        functools.partial(sublayer_kernel, same),
        out_shape=jax.ShapeDtypeStruct(x.shape, jnp.bfloat16),
        in_specs=[pl.BlockSpec(memory_space=pltpu.VMEM)] * 2,
        out_specs=pl.BlockSpec(memory_space=pltpu.VMEM),
        scratch_shapes=compute_scratch(tokens, width),
        compiler_params=pltpu.CompilerParams(vmem_limit_bytes=40 << 20),
    )(x, w)


def blocks_of(qkv, out, count):
    width = qkv.shape[0]
    return jnp.concatenate(
        [qkv.T.reshape(count, -1, width), out.T.reshape(count, -1, width)], axis=1
    )


def gathered(qkv, out):
    if lax.axis_size("seq") == HEADS:
        return lax.all_gather(blocks_of(qkv, out, 3), "seq", axis=0)
    full = blocks_of(
        lax.all_gather(qkv, "seq", axis=1, tiled=True),
        lax.all_gather(out, "seq", axis=1, tiled=True),
        3 * HEADS,
    )
    return full.reshape(HEADS, 3, *full.shape[1:])


def plain(video, spatial_qkv, spatial_out, temporal_qkv, temporal_out):
    frames_here, patches, width = video.shape
    n = lax.axis_size("seq")
    count = patches // n
    same_s = None if frames_here == 1 else same_by("div", patches)
    hidden = sublayer(video.reshape(-1, width), gathered(spatial_qkv, spatial_out), same_s)
    blocks = hidden.reshape(frames_here, n, count, width)
    received = lax.all_to_all(blocks, "seq", split_axis=1, concat_axis=0, tiled=True)
    result = sublayer(
        received.reshape(-1, width), gathered(temporal_qkv, temporal_out), same_by("mod", count)
    )
    positioned = result.reshape(frames_here * n, 1, count, width)
    returned = lax.all_to_all(positioned, "seq", split_axis=0, concat_axis=1, tiled=True)
    return returned.reshape(frames_here, patches, width)


RANKS = 4


def pair_of(value, j):
    if j == 0:
        return value
    if j == 1:
        return value + 1 - 2 * lax.rem(value, 2)
    if j == 2:
        return lax.rem(value + 2, 4)
    return 3 - value


def attended(i, at, table_ref, head, period=None):
    heads = table_ref.shape[0] // 3
    q, k = table_ref[i, at, :head], table_ref[heads + i, at, :head]
    v = table_ref[2 * heads + i, at]
    scores = lax.dot_general(k, q, (((0,), (0,)), ((), ())), preferred_element_type=jnp.float32)
    if period is not None:
        keys, queries = scores.shape
        a = lax.broadcasted_iota(jnp.int32, (1, period, queries), 1)
        b = lax.broadcasted_iota(jnp.int32, (1, period, queries), 2)
        parts = scores.reshape(keys // period, period, queries)
        scores = jnp.where(a == b % period, parts, -jnp.inf).reshape(keys, queries)
    centered = scores - jnp.max(scores, axis=0, keepdims=True)
    powers = jnp.exp2(centered * (math.log2(math.e) / math.sqrt(head))).astype(jnp.bfloat16)
    out = jnp.dot(v, powers, preferred_element_type=jnp.float32)
    return out[:head] * (1.0 / out[head : head + 1])


def fused_kernel(
    count, x_ref, sq_ref, so_ref, tq_ref, to_ref, out_ref,
    w_ref, na_ref, xt_ref, table_ref, ms_ref, mix_ref, nb_ref, g_ref, mt_ref, rs_ref, mr_ref,
    land_sem, deal_sem, line_sem, twin_sem, osib_sem, oy_sem, ox_sem, nland_sem, nsend_sem,
    msend_sem, mland_sem, asend_sem, gz_sem, fsend_sem, gr_sem, rsend_sem, rland_sem,
    x_vmem, keep_sem,
):
    n = HEADS
    me = lax.axis_index("seq")
    group = lax.axis_index("groups")
    z, r = lax.div(me, RANKS), lax.rem(me, RANKS)
    core, row = lax.rem(r, 2), lax.div(r, 2)
    side = lax.rem(group, 2)
    other = {"groups": group + 1 - 2 * side}
    sib = {"seq": RANKS * z + pair_of(r, 1)}
    far = {"seq": RANKS * z + pair_of(r, 2)}
    head = mix_ref.shape[1]
    width, tokens = xt_ref.shape
    wide = RANKS * head

    def move(src, dst, send, recv, device):
        return pltpu.make_async_remote_copy(
            src_ref=src, dst_ref=dst, send_sem=send, recv_sem=recv,
            device_id=device, device_id_type=MESH,
        )

    sends = []

    def go(*what):
        one = move(*what)
        one.start()
        sends.append(one)


    def slot_of(pair, b):
        if b == 0:
            return row + pair
        return (1 - pair) * (2 - 2 * row) + pair * (3 + r)

    def mine(zz, b):
        return slot_of(lax.rem(zz + side, 2), b)

    def theirs(zz, b):
        return slot_of(1 - lax.rem(zz + side, 2), b)

    def block(phase, zz, slot, send, device):
        at = w_ref.at[phase, zz, slot]
        return move(at, at, send, land_sem.at[phase, zz, slot], device)

    def landed(phase, zz, slot):
        block(phase, zz, slot, deal_sem.at[0, 0], other).wait_recv()

    def line(phase, zz, b, way):
        device = {"seq": me + RANKS * (1 - 2 * way)}
        return block(phase, zz, mine(zz, b), line_sem.at[phase, way, zz, b], device)

    def twin(phase, zz, b):
        return block(phase, zz, mine(zz, b), twin_sem.at[phase, zz, b], other)

    def keep(phase, q_ref, o_ref):
        slot = lax.div(3 * r + 2 * core, RANKS)
        return (
            pltpu.make_async_copy(q_ref.at[2 * core], w_ref.at[phase, z, slot], keep_sem.at[phase, 0]),
            pltpu.make_async_copy(o_ref.at[0], w_ref.at[phase, z, 3 + r], keep_sem.at[phase, 1]),
        )

    def deal(phase, q_ref):
        for which, j, device in ((0, 2 - 2 * core, far), (1, 1, sib)):
            slot = lax.div(3 * r + j, RANKS)
            go(
                q_ref.at[j], w_ref.at[phase, z, slot], deal_sem.at[phase, which],
                land_sem.at[phase, z, slot], device,
            )

    def along(phase, b):
        j, source = (1, pair_of(r, 1)) if b == 0 else (2 - 2 * core, pair_of(r, 2))
        landed(phase, z, lax.div(3 * source + j, RANKS))

        @pl.when(z < RANKS - 1)
        def _():
            line(phase, z, b, 0).start()

        @pl.when(z > 0)
        def _():
            line(phase, z, b, 1).start()

    def onward(phase, zz, b):
        twin(phase, zz, b).start()
        if b == 1:

            @pl.when(lax.rem(zz + side, 2) == 1)
            def _():
                out_first(phase, zz)

    def hop(phase, d, b, pair=None):
        def wanted(zz):
            return True if pair is None else lax.rem(zz + side, 2) == pair

        @pl.when((z >= d) & wanted(z + RANKS - d))
        def _():
            landed(phase, z - d, mine(z - d, b))

            @pl.when(z < RANKS - 1)
            def _():
                line(phase, z - d, b, 0).start()

            onward(phase, z - d, b)

        @pl.when((z + d < RANKS) & wanted(z + d))
        def _():
            landed(phase, z + d, mine(z + d, b))

            @pl.when(z > 0)
            def _():
                line(phase, z + d, b, 1).start()

            onward(phase, z + d, b)

    def from_twin(phase, zz, *which):
        for b in which:
            landed(phase, zz, theirs(zz, b))


    def beside(phase, zz, which, rank):
        return block(phase, zz, 3 + rank, osib_sem.at[phase, zz, which], sib)

    def over(phase, zz, rank, sem, device):
        return block(phase, zz, 3 + rank, sem.at[phase, lax.div(zz, 2)], device)

    def out_first(phase, zz):
        over(phase, zz, r, oy_sem, far).start()
        beside(phase, zz, 0, r).start()

    def out_own(phase):
        @pl.when(lax.rem(z + side, 2) == 1)
        def _():
            out_first(phase, z)

        @pl.when(lax.rem(z + side, 2) == 0)
        def _():
            beside(phase, z, 0, r).start()

    def out_twin(phase, j):
        zz = pair_of(z, j)
        from_twin(phase, zz, 1)

        @pl.when(lax.rem(zz + side, 2) == 0)
        def _():
            beside(phase, zz, 0, r).start()

    def out_second(phase, k):
        zz, rank = 2 * k + 1 - side, pair_of(r, 2)
        landed(phase, zz, 3 + rank)
        over(phase, zz, rank, ox_sem, other).start()
        beside(phase, zz, 1, rank).start()

    def out_third(phase, k):
        zz, rank = 2 * k + side, pair_of(r, 2)
        landed(phase, zz, 3 + rank)
        beside(phase, zz, 1, rank).start()

    def out_last(phase):
        for zz in range(RANKS):
            landed(phase, zz, 3 + pair_of(r, 1))
            landed(phase, zz, 3 + pair_of(r, 3))


    def normed(f, which, device):
        at = na_ref.at[f]
        return move(at, at, nsend_sem.at[which], nland_sem.at[f], device)

    def share(f, which, device):
        one = normed(f, which, device)
        one.start()
        sends.append(one)

    def project(zz, *frames):
        for f in frames:
            out = jnp.dot(
                w_ref[0, zz, 0:3].reshape(3 * head, width), na_ref[f],
                preferred_element_type=jnp.float32,
            )
            for slot in range(3):
                piece = out[slot * head : (slot + 1) * head]
                table_ref[3 * zz + slot, f, :head] = piece.astype(jnp.bfloat16)

    def project_all(zz):
        @pl.loop(0, RANKS)
        def _(f):
            project(zz, f)

    def spatial_head(i):
        @pl.loop(0, 2)
        def _(t):
            for f in (2 * t, 2 * t + 1):
                ms_ref[i, f] = attended(i, f, table_ref, head).astype(jnp.bfloat16)

        for j in (2, 3, 1):
            f = pair_of(r, j)
            go(
                ms_ref.at[i, f], mix_ref.at[RANKS * i + r], msend_sem.at[i, j],
                mland_sem.at[RANKS * i + r], {"seq": RANKS * z + f},
            )
        mix_ref[RANKS * i + r] = ms_ref[i, r]

    def mixed():
        for j in range(1, RANKS):
            for i in range(RANKS):
                h = RANKS * i + pair_of(r, j)
                move(
                    ms_ref.at[0, 0], mix_ref.at[h], msend_sem.at[0, 1], mland_sem.at[h], other
                ).wait_recv()

    def project_back(phase):
        @pl.loop(0, RANKS)
        def _(zz):
            update = jnp.dot(
                w_ref[phase, zz, 3:7].reshape(wide, width), mix_ref[...].reshape(width, tokens),
                preferred_element_type=jnp.float32,
            )
            at = pl.ds(pl.multiple_of(zz * wide, 8), wide)
            xt_ref[at, :] = xt_ref[at, :] + update

    def normalize_again():
        values = xt_ref[...].astype(jnp.bfloat16).astype(jnp.float32)
        xt_ref[...] = values
        centered = values - jnp.mean(values, axis=0, keepdims=True)
        spread = jnp.mean(centered * centered, axis=0, keepdims=True)
        nb_ref[...] = (centered * lax.rsqrt(spread + epsilon)).T.astype(jnp.bfloat16)


    def rows(zz, part):
        return pl.ds(pl.multiple_of((RANKS * zz + part) * count, count), count)

    def scatter():
        for part in range(RANKS):
            for j in range(1, RANKS):
                to = pair_of(z, j)
                go(
                    nb_ref.at[rows(to, part)], g_ref.at[part, RANKS * r + z],
                    asend_sem.at[part, j], gz_sem.at[part, z], {"seq": RANKS * to + r},
                )
        for part in range(RANKS):
            g_ref[part, RANKS * r + z] = nb_ref[rows(z, part), :]

    def frames(part, rank, which, device):
        at = g_ref.at[part, pl.ds(RANKS * rank, RANKS)]
        return move(at, at, fsend_sem.at[part, which], gr_sem.at[part, rank], device)

    def forward(part):
        for j in range(1, RANKS):
            source = pair_of(z, j)
            move(
                nb_ref.at[rows(0, 0)], g_ref.at[part, RANKS * r + source],
                asend_sem.at[0, 1], gz_sem.at[part, source], other,
            ).wait_recv()
        frames(part, r, 1, far).start()
        frames(part, r, 0, sib).start()

    def relay(part):
        rank = pair_of(r, 2)
        frames(part, rank, 0, sib).wait_recv()
        frames(part, rank, 2, sib).start()

    def ready(part):
        for j in (1, 3):
            frames(part, pair_of(r, j), 0, sib).wait_recv()

    def temporal(part):
        out = lax.dot_general(
            w_ref[1, :, 0:3].reshape(3 * wide, width), g_ref[part].reshape(tokens, width),
            (((1,), (1,)), ((), ())), preferred_element_type=jnp.float32,
        )
        for slot in range(3 * RANKS):
            piece = out[slot * head : (slot + 1) * head]
            table_ref[slot, part, :head] = piece.astype(jnp.bfloat16)

    def temporal_heads(part):
        @pl.loop(0, 2)
        def _(t):
            for i in (2 * t, 2 * t + 1):
                at = pl.ds(pl.multiple_of(i * head, 8), head)
                mt_ref[at, :] = attended(i, part, table_ref, head, count)

        rs_ref[part] = mt_ref[...].T.astype(jnp.bfloat16).reshape(rs_ref.shape[1:])

    def back(part, j):
        to = lax.rem(me + j, n)
        zt, rt = lax.div(to, RANKS), lax.rem(to, RANKS)
        return move(
            rs_ref.at[part, RANKS * rt + zt], mr_ref.at[r, RANKS * z + part],
            rsend_sem.at[part, j], rland_sem.at[r, RANKS * z + part], {"seq": to},
        )

    def returned():
        for j in range(1, n):
            source = lax.rem(me + j, n)
            zt, rt = lax.div(source, RANKS), lax.rem(source, RANKS)
            for part in range(RANKS):
                move(
                    rs_ref.at[0, 0], mr_ref.at[rt, RANKS * zt + part],
                    rsend_sem.at[0, 1], rland_sem.at[rt, RANKS * zt + part], other,
                ).wait_recv()
        for rank in range(RANKS):
            turned = mr_ref[rank].reshape(tokens, -1).astype(jnp.float32).T
            for i in range(RANKS):
                piece = turned[i * head : (i + 1) * head]
                mix_ref[RANKS * i + rank] = piece.astype(jnp.bfloat16)

    barrier = pltpu.get_barrier_semaphore()
    for j in range(1, n):
        pl.semaphore_signal(
            barrier, inc=1, device_id={"seq": lax.rem(me + j, n)}, device_id_type=MESH
        )
    pl.semaphore_signal(barrier, inc=1, device_id=other, device_id_type=MESH)
    copies = [pltpu.make_async_copy(x_ref, x_vmem, keep_sem.at[2, 0])]
    copies += [*keep(0, sq_ref, so_ref), *keep(1, tq_ref, to_ref)]
    for one in copies:
        one.start()
    table_ref[2 * RANKS :, :, head:, :] = jnp.ones_like(table_ref[2 * RANKS :, :, head:, :])
    mt_ref[...] = jnp.zeros_like(mt_ref)
    copies[0].wait()
    pl.semaphore_wait(barrier, n)

    one, two, three = (pair_of(r, j) for j in (1, 2, 3))
    near = [pair_of(z, j) for j in range(RANKS)]
    deal(0, sq_ref)
    for each in copies[1:]:
        each.wait()
    along(0, 0)
    normalize_into(x_vmem, xt_ref, na_ref.at[r])
    share(r, 1, far)
    share(r, 0, sib)
    along(0, 1)
    deal(1, tq_ref)
    hop(0, 1, 0)
    normed(one, 0, sib).wait_recv()
    project(z, r, one)
    hop(0, 2, 0)
    from_twin(0, near[1], 0)
    out_own(0)
    hop(0, 3, 0)
    for pair in range(2):
        for d in (1, 2):
            hop(0, d, 1, pair)
    along(1, 0)
    normed(two, 0, sib).wait_recv()
    share(two, 2, sib)
    along(1, 1)
    out_twin(0, 1)
    project(near[1], r, one)
    normed(three, 0, sib).wait_recv()
    project(z, two, three)
    project(near[1], two, three)
    hop(0, 3, 1)
    from_twin(0, near[2], 0)
    out_twin(0, 2)
    project_all(near[2])
    hop(1, 1, 0)
    from_twin(0, near[3], 0)
    out_twin(0, 3)
    project_all(near[3])
    hop(1, 2, 0)
    out_second(0, 0)
    out_second(0, 1)
    spatial_head(0)
    hop(1, 3, 0)
    out_third(0, 0)
    out_third(0, 1)
    spatial_head(1)
    for d in (1, 2):
        hop(1, d, 1, 0)
    spatial_head(2)
    for d in (1, 2):
        hop(1, d, 1, 1)
    spatial_head(3)
    mixed()
    out_last(0)
    project_back(0)
    normalize_again()
    scatter()
    hop(1, 3, 1)
    out_own(1)
    forward(0)
    for j in range(1, RANKS):
        from_twin(1, near[j], 0)
        out_twin(1, j)
    forward(1)
    relay(0)

    @pl.loop(0, RANKS)
    def _(part):
        ready(part)

        @pl.when(part < RANKS - 2)
        def _():
            forward(part + 2)

        temporal(part)

        @pl.when(part < RANKS - 1)
        def _():
            relay(part + 1)

        @pl.when(part == 1)
        def _():
            out_second(1, 0)
            out_second(1, 1)

        @pl.when(part == 2)
        def _():
            out_third(1, 0)
            out_third(1, 1)

        temporal_heads(part)
        for j in range(1, n):
            back(part, j).start()
        mr_ref[r, RANKS * z + part] = rs_ref[part, RANKS * r + z]

    out_last(1)
    returned()
    project_back(1)
    out_ref[...] = xt_ref[...].T.astype(jnp.bfloat16)

    for one in sends:
        one.wait_send()
    for phase in range(2):
        for b in range(2):
            for zz in range(RANKS):

                @pl.when((z >= zz) & (z < RANKS - 1))
                def _():
                    line(phase, zz, b, 0).wait_send()

                @pl.when((z <= zz) & (z > 0))
                def _():
                    line(phase, zz, b, 1).wait_send()

            for j in range(1, RANKS):
                twin(phase, near[j], b).wait_send()
        for k in range(2):
            over(phase, 2 * k + 1 - side, r, oy_sem, far).wait_send()
            over(phase, 2 * k + 1 - side, two, ox_sem, other).wait_send()
        for zz in range(RANKS):
            beside(phase, zz, 0, r).wait_send()
            beside(phase, zz, 1, two).wait_send()

    @pl.loop(0, RANKS)
    def _(part):
        for which, rank in ((0, r), (1, r), (2, pair_of(r, 2))):
            frames(part, rank, which, sib).wait_send()
        for j in range(1, n):
            back(part, j).wait_send()


def fused(video, spatial_qkv, spatial_out, temporal_qkv, temporal_out):
    _, tokens, width = video.shape
    n = lax.axis_size("seq")
    head, count = width // HEADS, tokens // n
    padded = -(-RANKS * head // 128) * 128
    vmem, dma = pltpu.VMEM, pltpu.SemaphoreType.DMA
    half = jnp.bfloat16

    def blocks(w):
        return w.T.reshape(-1, head, width)

    out = pl.pallas_call(
        functools.partial(fused_kernel, count),
        out_shape=jax.ShapeDtypeStruct((tokens, width), half),
        in_specs=[pl.BlockSpec(memory_space=pl.ANY)] * 5,
        out_specs=pl.BlockSpec(memory_space=pltpu.VMEM),
        scratch_shapes=[
            vmem((2, RANKS, 3 + RANKS, head, width), half),
            vmem((RANKS, width, tokens), half),
            vmem((width, tokens), jnp.float32),
            vmem((3 * RANKS, RANKS, head + 8, tokens), half),
            vmem((RANKS, RANKS, head, tokens), half),
            vmem((HEADS, head, tokens), half),
            vmem((tokens, width), half),
            vmem((RANKS, n, count, width), half),
            vmem((padded, tokens), jnp.float32),
            vmem((RANKS, n, count, padded), half),
            vmem((RANKS, n, count, padded), half),
            dma((2, RANKS, 3 + RANKS)),
            dma((2, 2)),
            dma((2, 2, RANKS, 2)),
            dma((2, RANKS, 2)),
            dma((2, RANKS, 2)),
            dma((2, 2)),
            dma((2, 2)),
            dma((RANKS,)),
            dma((3,)),
            dma((RANKS, RANKS)),
            dma((HEADS,)),
            dma((RANKS, RANKS)),
            dma((RANKS, RANKS)),
            dma((RANKS, 3)),
            dma((RANKS, RANKS)),
            dma((RANKS, n)),
            dma((RANKS, n)),
            vmem((tokens, width), half),
            dma((3, 2)),
        ],
        compiler_params=pltpu.CompilerParams(
            collective_id=0, has_side_effects=True, vmem_limit_bytes=60 << 20
        ),
    )(
        video.reshape(tokens, width),
        blocks(spatial_qkv), blocks(spatial_out), blocks(temporal_qkv), blocks(temporal_out),
    )
    return out.reshape(video.shape)


def local(video, spatial_qkv, *rest):
    n, groups = lax.axis_size("seq"), lax.axis_size("groups")
    frames_here, patches, _ = video.shape
    ringed = n == HEADS and groups % 2 == 0 and frames_here == 1 and patches % (16 * n) == 0
    return (fused if ringed else plain)(video, spatial_qkv, *rest)


def solution(mesh):
    split = P(None, "seq")
    placed = (P(("groups", "seq"), None, None), split, split, split, split)
    return jax.shard_map(
        local,
        mesh=mesh,
        in_specs=placed,
        out_specs=placed[0],
        check_vma=False,
    )
```

```python
import functools
import math

import jax
import jax.numpy as jnp
from jax import lax
from jax.experimental import pallas as pl
from jax.experimental.pallas import tpu as pltpu
from jax.sharding import PartitionSpec as P

HEADS = 16
epsilon = 1e-06
MESH = pl.DeviceIdType.MESH


def normalize_into(x_ref, xt_ref, nt_ref):
    xt_ref[...] = x_ref[...].astype(jnp.float32).T
    values = xt_ref[...]
    centered = values - jnp.mean(values, axis=0, keepdims=True)
    spread = jnp.mean(centered * centered, axis=0, keepdims=True)
    nt_ref[...] = (centered * lax.rsqrt(spread + epsilon)).astype(jnp.bfloat16)


def project_shard(w_ref, shard, nt_ref, table_ref):
    blocks, rows, width = w_ref.shape[1:]
    head = table_ref.shape[1]
    out = jnp.dot(
        w_ref[shard].reshape(blocks * rows, width), nt_ref[...], preferred_element_type=jnp.float32
    ).astype(jnp.bfloat16)
    for j in range(blocks):
        table_ref[shard * blocks + j] = out[j * rows : j * rows + head]


def attend_pair(pair, table_ref, mixed_ref, same, low=0, high=None):
    head = table_ref.shape[1]
    parts = []
    for j in range(2):
        h = pair * 2 + j
        q, k, v = table_ref[h, :, low:high], table_ref[HEADS + h], table_ref[2 * HEADS + h]
        scores = lax.dot_general(
            k, q, (((0,), (0,)), ((), ())), preferred_element_type=jnp.float32
        ) * (1.0 / math.sqrt(head))
        if same is not None:
            scores = jnp.where(same(scores.shape), scores, -jnp.inf)
        powers = jnp.exp(scores - jnp.max(scores, axis=0, keepdims=True))
        total = jnp.sum(powers, axis=0, keepdims=True)
        probs = (powers * (1.0 / total)).astype(jnp.bfloat16)
        parts.append(jnp.dot(v, probs, preferred_element_type=jnp.float32))
    both = jnp.concatenate(parts, axis=0).astype(jnp.bfloat16)
    mixed_ref[pl.ds(pl.multiple_of(pair * 2 * head, 16), 2 * head), low:high] = both


def project_out(w_ref, mixed_ref, xt_ref, out_ref, head, first=0, last=None):
    shards, blocks, rows, width = w_ref.shape
    low = head // 16 * 16
    step = 4
    tokens = slice(first, last)

    @pl.loop(0, shards // step)
    def _(i):
        weights = w_ref[pl.ds(i * step, step), :, low:, :].reshape(-1, width)
        update = jnp.dot(weights, mixed_ref[:, tokens], preferred_element_type=jnp.float32)
        update = update.reshape(step * blocks, rows - low, -1)[:, head - low :]
        count = step * blocks * (rows - head)
        at = pl.ds(pl.multiple_of(i * count, 8), count)
        xt_ref[at, tokens] = xt_ref[at, tokens] + update.reshape(count, -1)

    out_ref[tokens, :] = xt_ref[:, tokens].T.astype(jnp.bfloat16)


def same_by(kind, size):
    def same(shape):
        a = lax.broadcasted_iota(jnp.int32, shape, 0)
        b = lax.broadcasted_iota(jnp.int32, shape, 1)
        return (a % size == b % size) if kind == "mod" else (a // size == b // size)

    return same


def sublayer_kernel(same, x_ref, w_ref, out_ref, xt_ref, nt_ref, table_ref, mixed_ref):
    normalize_into(x_ref, xt_ref, nt_ref)

    @pl.loop(0, w_ref.shape[0])
    def _(d):
        project_shard(w_ref, d, nt_ref, table_ref)

    @pl.loop(0, HEADS // 2)
    def _(pair):
        attend_pair(pair, table_ref, mixed_ref, same)

    project_out(w_ref, mixed_ref, xt_ref, out_ref, table_ref.shape[1])


def compute_scratch(tokens, width):
    return [
        pltpu.VMEM((width, tokens), jnp.float32),
        pltpu.VMEM((width, tokens), jnp.bfloat16),
        pltpu.VMEM((3 * HEADS, width // HEADS, tokens), jnp.bfloat16),
        pltpu.VMEM((width, tokens), jnp.bfloat16),
    ]


def sublayer(x, w, same):
    tokens, width = x.shape
    return pl.pallas_call(
        functools.partial(sublayer_kernel, same),
        out_shape=jax.ShapeDtypeStruct(x.shape, jnp.bfloat16),
        in_specs=[pl.BlockSpec(memory_space=pltpu.VMEM)] * 2,
        out_specs=pl.BlockSpec(memory_space=pltpu.VMEM),
        scratch_shapes=compute_scratch(tokens, width),
        compiler_params=pltpu.CompilerParams(vmem_limit_bytes=40 << 20),
    )(x, w)


def blocks_of(qkv, out, count):
    width = qkv.shape[0]
    return jnp.concatenate(
        [qkv.T.reshape(count, -1, width), out.T.reshape(count, -1, width)], axis=1
    )


def gathered(qkv, out):
    if lax.axis_size("seq") == HEADS:
        return lax.all_gather(blocks_of(qkv, out, 3), "seq", axis=0)
    full = blocks_of(
        lax.all_gather(qkv, "seq", axis=1, tiled=True),
        lax.all_gather(out, "seq", axis=1, tiled=True),
        3 * HEADS,
    )
    return full.reshape(HEADS, 3, *full.shape[1:])


def plain(video, spatial_qkv, spatial_out, temporal_qkv, temporal_out):
    frames_here, patches, width = video.shape
    n = lax.axis_size("seq")
    count = patches // n
    same_s = None if frames_here == 1 else same_by("div", patches)
    hidden = sublayer(video.reshape(-1, width), gathered(spatial_qkv, spatial_out), same_s)
    blocks = hidden.reshape(frames_here, n, count, width)
    received = lax.all_to_all(blocks, "seq", split_axis=1, concat_axis=0, tiled=True)
    result = sublayer(
        received.reshape(-1, width), gathered(temporal_qkv, temporal_out), same_by("mod", count)
    )
    positioned = result.reshape(frames_here * n, 1, count, width)
    returned = lax.all_to_all(positioned, "seq", split_axis=0, concat_axis=1, tiled=True)
    return returned.reshape(frames_here, patches, width)


RANKS = 4


def pair_of(value, j):
    if j == 0:
        return value
    if j == 1:
        return value + 1 - 2 * lax.rem(value, 2)
    if j == 2:
        return lax.rem(value + 2, 4)
    return 3 - value


def attended(i, at, table_ref, head, period=None):
    heads = table_ref.shape[0] // 3
    q, k = table_ref[i, at, :head], table_ref[heads + i, at, :head]
    v = table_ref[2 * heads + i, at]
    scores = lax.dot_general(k, q, (((0,), (0,)), ((), ())), preferred_element_type=jnp.float32)
    if period is not None:
        keys, queries = scores.shape
        a = lax.broadcasted_iota(jnp.int32, (1, period, queries), 1)
        b = lax.broadcasted_iota(jnp.int32, (1, period, queries), 2)
        parts = scores.reshape(keys // period, period, queries)
        scores = jnp.where(a == b % period, parts, -jnp.inf).reshape(keys, queries)
    centered = scores - jnp.max(scores, axis=0, keepdims=True)
    powers = jnp.exp2(centered * (math.log2(math.e) / math.sqrt(head))).astype(jnp.bfloat16)
    out = jnp.dot(v, powers, preferred_element_type=jnp.float32)
    return out[:head] * (1.0 / out[head : head + 1])


def fused_kernel(
    count, x_ref, sq_ref, so_ref, tq_ref, to_ref, out_ref,
    w_ref, na_ref, xt_ref, table_ref, ms_ref, mix_ref, nb_ref, g_ref, mt_ref, rs_ref, mr_ref,
    land_sem, deal_sem, line_sem, twin_sem, osib_sem, oy_sem, nland_sem, nsend_sem,
    msend_sem, mland_sem, asend_sem, gz_sem, fsend_sem, gr_sem, rsend_sem, rland_sem,
    x_vmem, keep_sem,
):
    n = HEADS
    me = lax.axis_index("seq")
    group = lax.axis_index("groups")
    z, r = lax.div(me, RANKS), lax.rem(me, RANKS)
    core, row = lax.rem(r, 2), lax.div(r, 2)
    side = lax.rem(group, 2)
    other = {"groups": group + 1 - 2 * side}
    sib = {"seq": RANKS * z + pair_of(r, 1)}
    far = {"seq": RANKS * z + pair_of(r, 2)}
    head = mix_ref.shape[1]
    width, tokens = xt_ref.shape
    wide = RANKS * head

    def move(src, dst, send, recv, device):
        return pltpu.make_async_remote_copy(
            src_ref=src, dst_ref=dst, send_sem=send, recv_sem=recv,
            device_id=device, device_id_type=MESH,
        )

    sends = []

    def go(*what):
        one = move(*what)
        one.start()
        sends.append(one)


    own_slot = lax.div(3 * r + 2 * core, RANKS)
    sib_slot = lax.div(3 * pair_of(r, 1) + 1, RANKS)
    far_slot = 2 - 2 * row

    def slot_of(phase, pair, b):
        if b == 0:
            return (1 - pair) * own_slot + pair * ((3 + r) if phase else sib_slot)
        return (1 - pair) * far_slot + pair * (sib_slot if phase else (3 + r))

    def mine(phase, zz, b):
        return slot_of(phase, lax.rem(zz + side, 2), b)

    def theirs(phase, zz, b):
        return slot_of(phase, 1 - lax.rem(zz + side, 2), b)

    def block(phase, zz, slot, send, device):
        at = w_ref.at[phase, zz, slot]
        return move(at, at, send, land_sem.at[phase, zz, slot], device)

    def landed(phase, zz, slot):
        block(phase, zz, slot, deal_sem.at[0, 0], other).wait_recv()

    def line(phase, zz, b, way):
        device = {"seq": me + RANKS * (1 - 2 * way)}
        return block(phase, zz, mine(phase, zz, b), line_sem.at[phase, way, zz, b], device)

    def twin(phase, zz, b):
        return block(phase, zz, mine(phase, zz, b), twin_sem.at[phase, zz, b], other)

    def keep(phase, q_ref, o_ref):
        return (
            pltpu.make_async_copy(q_ref.at[2 * core], w_ref.at[phase, z, own_slot], keep_sem.at[phase, 0]),
            pltpu.make_async_copy(o_ref.at[0], w_ref.at[phase, z, 3 + r], keep_sem.at[phase, 1]),
        )

    def deal(phase, q_ref):
        for which, j, device in ((0, 2 - 2 * core, far), (1, 1, sib)):
            slot = lax.div(3 * r + j, RANKS)
            go(
                q_ref.at[j], w_ref.at[phase, z, slot], deal_sem.at[phase, which],
                land_sem.at[phase, z, slot], device,
            )

    def along(phase, b):
        @pl.when(z < RANKS - 1)
        def _():
            line(phase, z, b, 0).start()

        @pl.when(z > 0)
        def _():
            line(phase, z, b, 1).start()

    def by_pair(zz, pair, run):
        @pl.when(lax.rem(zz + side, 2) == pair)
        def _():
            run()

    def onward(phase, zz, b):
        twin(phase, zz, b).start()
        if phase == 0 and b == 1:

            @pl.when(lax.rem(zz + side, 2) == 1)
            def _():
                out_first(phase, zz)

    def hop(phase, d, b, pair=None):
        def wanted(zz):
            return True if pair is None else lax.rem(zz + side, 2) == pair

        @pl.when((z >= d) & wanted(z + RANKS - d))
        def _():
            landed(phase, z - d, mine(phase, z - d, b))

            @pl.when(z < RANKS - 1)
            def _():
                line(phase, z - d, b, 0).start()

            onward(phase, z - d, b)

        @pl.when((z + d < RANKS) & wanted(z + d))
        def _():
            landed(phase, z + d, mine(phase, z + d, b))

            @pl.when(z > 0)
            def _():
                line(phase, z + d, b, 1).start()

            onward(phase, z + d, b)

    def from_twin(phase, zz, *which):
        for b in which:
            landed(phase, zz, theirs(phase, zz, b))


    def beside(phase, zz, which, rank):
        return block(phase, zz, 3 + rank, osib_sem.at[phase, zz, which], sib)

    def over(phase, zz):
        return block(phase, zz, 3 + r, oy_sem.at[phase, zz], far)

    def out_first(phase, zz):
        over(phase, zz).start()
        beside(phase, zz, 0, r).start()

    def out_twin(phase, zz):
        from_twin(phase, zz, 1 - phase)
        out_first(phase, zz)

    def out_relay(phase):
        for zz in range(RANKS):
            landed(phase, zz, 3 + pair_of(r, 2))
            beside(phase, zz, 1, pair_of(r, 2)).start()

    def out_last(phase):
        for zz in range(RANKS):
            landed(phase, zz, 3 + pair_of(r, 1))
            landed(phase, zz, 3 + pair_of(r, 3))


    def normed(f, which, device):
        at = na_ref.at[f]
        return move(at, at, nsend_sem.at[which], nland_sem.at[f], device)

    def share(f, which, device):
        one = normed(f, which, device)
        one.start()
        sends.append(one)

    def project(zz, *frames):
        for f in frames:
            out = jnp.dot(
                w_ref[0, zz, 0:3].reshape(3 * head, width), na_ref[f],
                preferred_element_type=jnp.float32,
            )
            for slot in range(3):
                piece = out[slot * head : (slot + 1) * head]
                table_ref[3 * zz + slot, f, :head] = piece.astype(jnp.bfloat16)

    def project_all(zz):
        @pl.loop(0, RANKS)
        def _(f):
            project(zz, f)

    def spatial_head(i):
        @pl.loop(0, 2)
        def _(t):
            for f in (2 * t, 2 * t + 1):
                ms_ref[i, f] = attended(i, f, table_ref, head).astype(jnp.bfloat16)

        for j in (2, 3, 1):
            f = pair_of(r, j)
            go(
                ms_ref.at[i, f], mix_ref.at[RANKS * i + r], msend_sem.at[i, j],
                mland_sem.at[RANKS * i + r], {"seq": RANKS * z + f},
            )
        mix_ref[RANKS * i + r] = ms_ref[i, r]

    def mixed():
        for j in range(1, RANKS):
            for i in range(RANKS):
                h = RANKS * i + pair_of(r, j)
                move(
                    ms_ref.at[0, 0], mix_ref.at[h], msend_sem.at[0, 1], mland_sem.at[h], other
                ).wait_recv()

    def project_back(phase):
        @pl.loop(0, RANKS)
        def _(zz):
            update = jnp.dot(
                w_ref[phase, zz, 3:7].reshape(wide, width), mix_ref[...].reshape(width, tokens),
                preferred_element_type=jnp.float32,
            )
            at = pl.ds(pl.multiple_of(zz * wide, 8), wide)
            xt_ref[at, :] = xt_ref[at, :] + update

    def normalize_again():
        values = xt_ref[...].astype(jnp.bfloat16).astype(jnp.float32)
        xt_ref[...] = values
        centered = values - jnp.mean(values, axis=0, keepdims=True)
        spread = jnp.mean(centered * centered, axis=0, keepdims=True)
        nb_ref[...] = (centered * lax.rsqrt(spread + epsilon)).T.astype(jnp.bfloat16)


    def rows(zz, part):
        return pl.ds(pl.multiple_of((RANKS * zz + part) * count, count), count)

    def scatter():
        for part in range(RANKS):
            for j in range(1, RANKS):
                to = pair_of(z, j)
                go(
                    nb_ref.at[rows(to, part)], g_ref.at[part, RANKS * r + z],
                    asend_sem.at[part, j], gz_sem.at[part, z], {"seq": RANKS * to + r},
                )
        for part in range(RANKS):
            g_ref[part, RANKS * r + z] = nb_ref[rows(z, part), :]

    def frames(part, rank, which, device):
        at = g_ref.at[part, pl.ds(RANKS * rank, RANKS)]
        return move(at, at, fsend_sem.at[part, which], gr_sem.at[part, rank], device)

    def forward(part):
        for j in range(1, RANKS):
            source = pair_of(z, j)
            move(
                nb_ref.at[rows(0, 0)], g_ref.at[part, RANKS * r + source],
                asend_sem.at[0, 1], gz_sem.at[part, source], other,
            ).wait_recv()
        frames(part, r, 1, far).start()
        frames(part, r, 0, sib).start()

    def relay(part):
        rank = pair_of(r, 2)
        frames(part, rank, 0, sib).wait_recv()
        frames(part, rank, 2, sib).start()

    def ready(part):
        for j in (1, 3):
            frames(part, pair_of(r, j), 0, sib).wait_recv()

    def temporal(part):
        out = lax.dot_general(
            w_ref[1, :, 0:3].reshape(3 * wide, width), g_ref[part].reshape(tokens, width),
            (((1,), (1,)), ((), ())), preferred_element_type=jnp.float32,
        )
        for slot in range(3 * RANKS):
            piece = out[slot * head : (slot + 1) * head]
            table_ref[slot, part, :head] = piece.astype(jnp.bfloat16)

    def temporal_heads(part):
        @pl.loop(0, 2)
        def _(t):
            for i in (2 * t, 2 * t + 1):
                at = pl.ds(pl.multiple_of(i * head, 8), head)
                mt_ref[at, :] = attended(i, part, table_ref, head, count)

        rs_ref[part] = mt_ref[...].T.astype(jnp.bfloat16).reshape(rs_ref.shape[1:])

    def back(part, j):
        to = lax.rem(me + j, n)
        zt, rt = lax.div(to, RANKS), lax.rem(to, RANKS)
        return move(
            rs_ref.at[part, RANKS * rt + zt], mr_ref.at[r, RANKS * z + part],
            rsend_sem.at[part, j], rland_sem.at[r, RANKS * z + part], {"seq": to},
        )

    def returned():
        for j in range(1, n):
            source = lax.rem(me + j, n)
            zt, rt = lax.div(source, RANKS), lax.rem(source, RANKS)
            for part in range(RANKS):
                move(
                    rs_ref.at[0, 0], mr_ref.at[rt, RANKS * zt + part],
                    rsend_sem.at[0, 1], rland_sem.at[rt, RANKS * zt + part], other,
                ).wait_recv()
        for rank in range(RANKS):
            turned = mr_ref[rank].reshape(tokens, -1).astype(jnp.float32).T
            for i in range(RANKS):
                piece = turned[i * head : (i + 1) * head]
                mix_ref[RANKS * i + rank] = piece.astype(jnp.bfloat16)

    barrier = pltpu.get_barrier_semaphore()
    greeted = [other, sib, far]
    for device in greeted:
        pl.semaphore_signal(barrier, inc=1, device_id=device, device_id_type=MESH)
    for inside, way in ((z < RANKS - 1, 1), (z > 0, -1)):

        @pl.when(inside)
        def _():
            device = {"seq": me + RANKS * way}
            pl.semaphore_signal(barrier, inc=1, device_id=device, device_id_type=MESH)

    copies = [pltpu.make_async_copy(x_ref, x_vmem, keep_sem.at[2, 0])]
    copies += [*keep(0, sq_ref, so_ref), *keep(1, tq_ref, to_ref)]
    for one in copies:
        one.start()
    table_ref[2 * RANKS :, :, head:, :] = jnp.ones_like(table_ref[2 * RANKS :, :, head:, :])
    mt_ref[...] = jnp.zeros_like(mt_ref)
    copies[0].wait()
    middle = (z > 0) & (z < RANKS - 1)
    pl.semaphore_wait(barrier, len(greeted) + 1 + lax.rem(lax.div(z + 1, 2), 2))


    one, two, three = (pair_of(r, j) for j in (1, 2, 3))
    near = [pair_of(z, j) for j in range(RANKS)]
    deal(0, sq_ref)
    for each in copies[1:3]:
        each.wait()
    by_pair(z, 0, lambda: along(0, 0))
    landed(0, z, sib_slot)
    by_pair(z, 1, lambda: along(0, 0))
    normalize_into(x_vmem, xt_ref, na_ref.at[r])
    share(r, 1, far)
    share(r, 0, sib)
    landed(0, z, far_slot)
    along(0, 1)
    deal(1, tq_ref)
    hop(0, 1, 0)
    normed(one, 0, sib).wait_recv()
    project(z, r, one)
    out_first(0, z)
    hop(0, 1, 1, 0)
    hop(0, 2, 0)
    from_twin(0, near[1], 0)
    hop(0, 3, 0)
    hop(0, 2, 1, 0)
    hop(0, 1, 1, 1)
    normed(two, 0, sib).wait_recv()
    share(two, 2, sib)

    @pl.when(middle)
    def _():
        hop(0, 2, 1, 1)

    for each in copies[3:]:
        each.wait()
    landed(1, z, sib_slot)
    landed(1, z, far_slot)
    along(1, 0)
    along(1, 1)
    by_pair(near[1], 1, lambda: from_twin(0, near[1], 1))
    project(near[1], r, one)
    normed(three, 0, sib).wait_recv()
    project(z, two, three)
    project(near[1], two, three)
    from_twin(0, near[2], 0)
    by_pair(near[2], 1, lambda: from_twin(0, near[2], 1))
    project_all(near[2])
    hop(0, 3, 1, 0)

    @pl.when(jnp.logical_not(middle))
    def _():
        hop(0, 2, 1, 1)

    hop(0, 3, 1, 1)
    from_twin(0, near[3], 0)
    by_pair(near[3], 1, lambda: from_twin(0, near[3], 1))
    project_all(near[3])
    for j in (1, 2):
        by_pair(near[j], 0, lambda: out_twin(0, near[j]))
    hop(1, 1, 0)
    spatial_head(0)
    hop(1, 1, 1)
    spatial_head(1)
    by_pair(near[3], 0, lambda: out_twin(0, near[3]))
    hop(1, 2, 0)
    spatial_head(2)
    spatial_head(3)
    hop(1, 3, 0)
    out_first(1, z)
    for j in range(1, RANKS):
        by_pair(near[j], 1, lambda: out_first(1, near[j]))

    @pl.when(middle)
    def _():
        hop(1, 2, 1)

    out_relay(0)
    mixed()
    out_last(0)
    for j in range(1, RANKS):
        by_pair(near[j], 0, lambda: out_twin(1, near[j]))
    project_back(0)
    normalize_again()
    scatter()

    @pl.when(jnp.logical_not(middle))
    def _():
        hop(1, 2, 1)

    hop(1, 3, 1)
    forward(0)
    forward(1)
    for j in range(1, RANKS):
        by_pair(near[j], 1, lambda: from_twin(1, near[j], 0))
    relay(0)
    for j in range(1, RANKS):
        from_twin(1, near[j], 1)

    @pl.loop(0, RANKS)
    def _(part):
        ready(part)

        @pl.when(part < RANKS - 2)
        def _():
            forward(part + 2)

        temporal(part)

        @pl.when(part < RANKS - 1)
        def _():
            relay(part + 1)

        @pl.when(part == 1)
        def _():
            out_relay(1)

        temporal_heads(part)
        for j in range(1, n):
            back(part, j).start()
        mr_ref[r, RANKS * z + part] = rs_ref[part, RANKS * r + z]

    out_last(1)
    returned()
    project_back(1)
    out_ref[...] = xt_ref[...].T.astype(jnp.bfloat16)

    for one in sends:
        one.wait_send()
    for phase in range(2):
        for b in range(2):
            for zz in range(RANKS):

                @pl.when((z >= zz) & (z < RANKS - 1))
                def _():
                    line(phase, zz, b, 0).wait_send()

                @pl.when((z <= zz) & (z > 0))
                def _():
                    line(phase, zz, b, 1).wait_send()

            for j in range(1, RANKS):
                twin(phase, near[j], b).wait_send()
        for zz in range(RANKS):
            over(phase, zz).wait_send()
            beside(phase, zz, 0, r).wait_send()
            beside(phase, zz, 1, two).wait_send()

    @pl.loop(0, RANKS)
    def _(part):
        for which, rank in ((0, r), (1, r), (2, pair_of(r, 2))):
            frames(part, rank, which, sib).wait_send()
        for j in range(1, n):
            back(part, j).wait_send()


def fused(video, spatial_qkv, spatial_out, temporal_qkv, temporal_out):
    _, tokens, width = video.shape
    n = lax.axis_size("seq")
    head, count = width // HEADS, tokens // n
    padded = -(-RANKS * head // 128) * 128
    vmem, dma = pltpu.VMEM, pltpu.SemaphoreType.DMA
    half = jnp.bfloat16

    def blocks(w):
        return w.T.reshape(-1, head, width)

    out = pl.pallas_call(
        functools.partial(fused_kernel, count),
        out_shape=jax.ShapeDtypeStruct((tokens, width), half),
        in_specs=[pl.BlockSpec(memory_space=pl.ANY)] * 5,
        out_specs=pl.BlockSpec(memory_space=pltpu.VMEM),
        scratch_shapes=[
            vmem((2, RANKS, 3 + RANKS, head, width), half),
            vmem((RANKS, width, tokens), half),
            vmem((width, tokens), jnp.float32),
            vmem((3 * RANKS, RANKS, head + 8, tokens), half),
            vmem((RANKS, RANKS, head, tokens), half),
            vmem((HEADS, head, tokens), half),
            vmem((tokens, width), half),
            vmem((RANKS, n, count, width), half),
            vmem((padded, tokens), jnp.float32),
            vmem((RANKS, n, count, padded), half),
            vmem((RANKS, n, count, padded), half),
            dma((2, RANKS, 3 + RANKS)),
            dma((2, 2)),
            dma((2, 2, RANKS, 2)),
            dma((2, RANKS, 2)),
            dma((2, RANKS, 2)),
            dma((2, RANKS)),
            dma((RANKS,)),
            dma((3,)),
            dma((RANKS, RANKS)),
            dma((HEADS,)),
            dma((RANKS, RANKS)),
            dma((RANKS, RANKS)),
            dma((RANKS, 3)),
            dma((RANKS, RANKS)),
            dma((RANKS, n)),
            dma((RANKS, n)),
            vmem((tokens, width), half),
            dma((3, 2)),
        ],
        compiler_params=pltpu.CompilerParams(
            collective_id=0, has_side_effects=True, vmem_limit_bytes=60 << 20
        ),
    )(
        video.reshape(tokens, width),
        blocks(spatial_qkv), blocks(spatial_out), blocks(temporal_qkv), blocks(temporal_out),
    )
    return out.reshape(video.shape)


def local(video, spatial_qkv, *rest):
    n, groups = lax.axis_size("seq"), lax.axis_size("groups")
    frames_here, patches, _ = video.shape
    ringed = n == HEADS and groups % 2 == 0 and frames_here == 1 and patches % (16 * n) == 0
    return (fused if ringed else plain)(video, spatial_qkv, *rest)


def solution(mesh):
    split = P(None, "seq")
    placed = (P(("groups", "seq"), None, None), split, split, split, split)
    return jax.shard_map(
        local,
        mesh=mesh,
        in_specs=placed,
        out_specs=placed[0],
        check_vma=False,
    )
```

```python
import functools
import math

import jax
import jax.numpy as jnp
from jax import lax
from jax.experimental import pallas as pl
from jax.experimental.pallas import tpu as pltpu
from jax.sharding import PartitionSpec as P

HEADS = 16
epsilon = 1e-06
MESH = pl.DeviceIdType.MESH


def normalize_into(x_ref, xt_ref, nt_ref):
    xt_ref[...] = x_ref[...].astype(jnp.float32).T
    values = xt_ref[...]
    centered = values - jnp.mean(values, axis=0, keepdims=True)
    spread = jnp.mean(centered * centered, axis=0, keepdims=True)
    nt_ref[...] = (centered * lax.rsqrt(spread + epsilon)).astype(jnp.bfloat16)


def project_shard(w_ref, shard, nt_ref, table_ref):
    blocks, rows, width = w_ref.shape[1:]
    head = table_ref.shape[1]
    out = jnp.dot(
        w_ref[shard].reshape(blocks * rows, width), nt_ref[...], preferred_element_type=jnp.float32
    ).astype(jnp.bfloat16)
    for j in range(blocks):
        table_ref[shard * blocks + j] = out[j * rows : j * rows + head]


def attend_pair(pair, table_ref, mixed_ref, same, low=0, high=None):
    head = table_ref.shape[1]
    parts = []
    for j in range(2):
        h = pair * 2 + j
        q, k, v = table_ref[h, :, low:high], table_ref[HEADS + h], table_ref[2 * HEADS + h]
        scores = lax.dot_general(
            k, q, (((0,), (0,)), ((), ())), preferred_element_type=jnp.float32
        ) * (1.0 / math.sqrt(head))
        if same is not None:
            scores = jnp.where(same(scores.shape), scores, -jnp.inf)
        powers = jnp.exp(scores - jnp.max(scores, axis=0, keepdims=True))
        total = jnp.sum(powers, axis=0, keepdims=True)
        probs = (powers * (1.0 / total)).astype(jnp.bfloat16)
        parts.append(jnp.dot(v, probs, preferred_element_type=jnp.float32))
    both = jnp.concatenate(parts, axis=0).astype(jnp.bfloat16)
    mixed_ref[pl.ds(pl.multiple_of(pair * 2 * head, 16), 2 * head), low:high] = both


def project_out(w_ref, mixed_ref, xt_ref, out_ref, head, first=0, last=None):
    shards, blocks, rows, width = w_ref.shape
    low = head // 16 * 16
    step = 4
    tokens = slice(first, last)

    @pl.loop(0, shards // step)
    def _(i):
        weights = w_ref[pl.ds(i * step, step), :, low:, :].reshape(-1, width)
        update = jnp.dot(weights, mixed_ref[:, tokens], preferred_element_type=jnp.float32)
        update = update.reshape(step * blocks, rows - low, -1)[:, head - low :]
        count = step * blocks * (rows - head)
        at = pl.ds(pl.multiple_of(i * count, 8), count)
        xt_ref[at, tokens] = xt_ref[at, tokens] + update.reshape(count, -1)

    out_ref[tokens, :] = xt_ref[:, tokens].T.astype(jnp.bfloat16)


def same_by(kind, size):
    def same(shape):
        a = lax.broadcasted_iota(jnp.int32, shape, 0)
        b = lax.broadcasted_iota(jnp.int32, shape, 1)
        return (a % size == b % size) if kind == "mod" else (a // size == b // size)

    return same


def sublayer_kernel(same, x_ref, w_ref, out_ref, xt_ref, nt_ref, table_ref, mixed_ref):
    normalize_into(x_ref, xt_ref, nt_ref)

    @pl.loop(0, w_ref.shape[0])
    def _(d):
        project_shard(w_ref, d, nt_ref, table_ref)

    @pl.loop(0, HEADS // 2)
    def _(pair):
        attend_pair(pair, table_ref, mixed_ref, same)

    project_out(w_ref, mixed_ref, xt_ref, out_ref, table_ref.shape[1])


def compute_scratch(tokens, width):
    return [
        pltpu.VMEM((width, tokens), jnp.float32),
        pltpu.VMEM((width, tokens), jnp.bfloat16),
        pltpu.VMEM((3 * HEADS, width // HEADS, tokens), jnp.bfloat16),
        pltpu.VMEM((width, tokens), jnp.bfloat16),
    ]


def sublayer(x, w, same):
    tokens, width = x.shape
    return pl.pallas_call(
        functools.partial(sublayer_kernel, same),
        out_shape=jax.ShapeDtypeStruct(x.shape, jnp.bfloat16),
        in_specs=[pl.BlockSpec(memory_space=pltpu.VMEM)] * 2,
        out_specs=pl.BlockSpec(memory_space=pltpu.VMEM),
        scratch_shapes=compute_scratch(tokens, width),
        compiler_params=pltpu.CompilerParams(vmem_limit_bytes=40 << 20),
    )(x, w)


def blocks_of(qkv, out, count):
    width = qkv.shape[0]
    return jnp.concatenate(
        [qkv.T.reshape(count, -1, width), out.T.reshape(count, -1, width)], axis=1
    )


def gathered(qkv, out):
    if lax.axis_size("seq") == HEADS:
        return lax.all_gather(blocks_of(qkv, out, 3), "seq", axis=0)
    full = blocks_of(
        lax.all_gather(qkv, "seq", axis=1, tiled=True),
        lax.all_gather(out, "seq", axis=1, tiled=True),
        3 * HEADS,
    )
    return full.reshape(HEADS, 3, *full.shape[1:])


def plain(video, spatial_qkv, spatial_out, temporal_qkv, temporal_out):
    frames_here, patches, width = video.shape
    n = lax.axis_size("seq")
    count = patches // n
    same_s = None if frames_here == 1 else same_by("div", patches)
    hidden = sublayer(video.reshape(-1, width), gathered(spatial_qkv, spatial_out), same_s)
    blocks = hidden.reshape(frames_here, n, count, width)
    received = lax.all_to_all(blocks, "seq", split_axis=1, concat_axis=0, tiled=True)
    result = sublayer(
        received.reshape(-1, width), gathered(temporal_qkv, temporal_out), same_by("mod", count)
    )
    positioned = result.reshape(frames_here * n, 1, count, width)
    returned = lax.all_to_all(positioned, "seq", split_axis=0, concat_axis=1, tiled=True)
    return returned.reshape(frames_here, patches, width)


RANKS = 4


def pair_of(value, j):
    if j == 0:
        return value
    if j == 1:
        return value + 1 - 2 * lax.rem(value, 2)
    if j == 2:
        return lax.rem(value + 2, 4)
    return 3 - value


def attended(i, at, table_ref, head, period=None):
    heads = table_ref.shape[0] // 3
    q, k = table_ref[i, at, :head], table_ref[heads + i, at, :head]
    v = table_ref[2 * heads + i, at]
    scores = lax.dot_general(k, q, (((0,), (0,)), ((), ())), preferred_element_type=jnp.float32)
    if period is not None:
        keys, queries = scores.shape
        a = lax.broadcasted_iota(jnp.int32, (1, period, queries), 1)
        b = lax.broadcasted_iota(jnp.int32, (1, period, queries), 2)
        parts = scores.reshape(keys // period, period, queries)
        scores = jnp.where(a == b % period, parts, -jnp.inf).reshape(keys, queries)
    centered = scores - jnp.max(scores, axis=0, keepdims=True)
    powers = jnp.exp2(centered * (math.log2(math.e) / math.sqrt(head))).astype(jnp.bfloat16)
    out = jnp.dot(v, powers, preferred_element_type=jnp.float32)
    return out[:head] * (1.0 / out[head : head + 1])


def fused_kernel(
    count, x_ref, sq_ref, so_ref, tq_ref, to_ref, out_ref,
    w_ref, na_ref, xt_ref, table_ref, ms_ref, mix_ref, nb_ref, g_ref, mt_ref, rs_ref, mr_ref,
    land_sem, deal_sem, line_sem, twin_sem, osib_sem, oy_sem, nland_sem, nsend_sem,
    msend_sem, mland_sem, asend_sem, gz_sem, fsend_sem, gr_sem, rsend_sem, rland_sem,
    x_vmem, keep_sem,
):
    n = HEADS
    me = lax.axis_index("seq")
    group = lax.axis_index("groups")
    z, r = lax.div(me, RANKS), lax.rem(me, RANKS)
    core, row = lax.rem(r, 2), lax.div(r, 2)
    side = lax.rem(group, 2)
    other = {"groups": group + 1 - 2 * side}
    sib = {"seq": RANKS * z + pair_of(r, 1)}
    far = {"seq": RANKS * z + pair_of(r, 2)}
    head = mix_ref.shape[1]
    width, tokens = xt_ref.shape
    wide = RANKS * head

    def move(src, dst, send, recv, device):
        return pltpu.make_async_remote_copy(
            src_ref=src, dst_ref=dst, send_sem=send, recv_sem=recv,
            device_id=device, device_id_type=MESH,
        )

    sends = []

    def go(*what):
        one = move(*what)
        one.start()
        sends.append(one)


    own_slot = lax.div(3 * r + 2 * core, RANKS)
    sib_slot = lax.div(3 * pair_of(r, 1) + 1, RANKS)
    far_slot = 2 - 2 * row

    def slot_of(phase, pair, b):
        if b == 0:
            return (1 - pair) * own_slot + pair * ((3 + r) if phase else sib_slot)
        return (1 - pair) * far_slot + pair * (sib_slot if phase else (3 + r))

    def mine(phase, zz, b):
        return slot_of(phase, lax.rem(zz + side, 2), b)

    def theirs(phase, zz, b):
        return slot_of(phase, 1 - lax.rem(zz + side, 2), b)

    def block(phase, zz, slot, send, device):
        at = w_ref.at[phase, zz, slot]
        return move(at, at, send, land_sem.at[phase, zz, slot], device)

    def landed(phase, zz, slot):
        block(phase, zz, slot, deal_sem.at[0, 0], other).wait_recv()

    def line(phase, zz, b, way):
        device = {"seq": me + RANKS * (1 - 2 * way)}
        return block(phase, zz, mine(phase, zz, b), line_sem.at[phase, way, zz, b], device)

    def twin(phase, zz, b):
        return block(phase, zz, mine(phase, zz, b), twin_sem.at[phase, zz, b], other)

    def keep(phase, q_ref, o_ref):
        return (
            pltpu.make_async_copy(q_ref.at[2 * core], w_ref.at[phase, z, own_slot], keep_sem.at[phase, 0]),
            pltpu.make_async_copy(o_ref.at[0], w_ref.at[phase, z, 3 + r], keep_sem.at[phase, 1]),
        )

    def deal(phase, q_ref):
        for which, j, device in ((0, 2 - 2 * core, far), (1, 1, sib)):
            slot = lax.div(3 * r + j, RANKS)
            go(
                q_ref.at[j], w_ref.at[phase, z, slot], deal_sem.at[phase, which],
                land_sem.at[phase, z, slot], device,
            )

    def along(phase, b):
        @pl.when(z < RANKS - 1)
        def _():
            line(phase, z, b, 0).start()

        @pl.when(z > 0)
        def _():
            line(phase, z, b, 1).start()

    def by_pair(zz, pair, run):
        @pl.when(lax.rem(zz + side, 2) == pair)
        def _():
            run()

    def onward(phase, zz, b):
        twin(phase, zz, b).start()
        if phase == 0 and b == 1:

            @pl.when(lax.rem(zz + side, 2) == 1)
            def _():
                out_first(phase, zz)

    def hop(phase, d, b, pair=None):
        def wanted(zz):
            return True if pair is None else lax.rem(zz + side, 2) == pair

        @pl.when((z >= d) & wanted(z + RANKS - d))
        def _():
            landed(phase, z - d, mine(phase, z - d, b))

            @pl.when(z < RANKS - 1)
            def _():
                line(phase, z - d, b, 0).start()

            onward(phase, z - d, b)

        @pl.when((z + d < RANKS) & wanted(z + d))
        def _():
            landed(phase, z + d, mine(phase, z + d, b))

            @pl.when(z > 0)
            def _():
                line(phase, z + d, b, 1).start()

            onward(phase, z + d, b)

    def from_twin(phase, zz, *which):
        for b in which:
            landed(phase, zz, theirs(phase, zz, b))


    def beside(phase, zz, which, rank):
        return block(phase, zz, 3 + rank, osib_sem.at[phase, zz, which], sib)

    def over(phase, zz):
        return block(phase, zz, 3 + r, oy_sem.at[phase, zz], far)

    def out_first(phase, zz):
        over(phase, zz).start()
        beside(phase, zz, 0, r).start()

    def out_twin(phase, zz):
        from_twin(phase, zz, 1 - phase)
        out_first(phase, zz)

    def out_relay(phase):
        for zz in range(RANKS):
            landed(phase, zz, 3 + pair_of(r, 2))
            beside(phase, zz, 1, pair_of(r, 2)).start()

    def out_last(phase):
        for zz in range(RANKS):
            landed(phase, zz, 3 + pair_of(r, 1))
            landed(phase, zz, 3 + pair_of(r, 3))


    def normed(f, which, device):
        at = na_ref.at[f]
        return move(at, at, nsend_sem.at[which], nland_sem.at[f], device)

    def share(f, which, device):
        one = normed(f, which, device)
        one.start()
        sends.append(one)

    def project(zz, *frames):
        for f in frames:
            out = jnp.dot(
                w_ref[0, zz, 0:3].reshape(3 * head, width), na_ref[f],
                preferred_element_type=jnp.float32,
            )
            for slot in range(3):
                piece = out[slot * head : (slot + 1) * head]
                table_ref[3 * zz + slot, f, :head] = piece.astype(jnp.bfloat16)

    def project_all(zz):
        @pl.loop(0, RANKS)
        def _(f):
            project(zz, f)

    def spatial_head(i):
        @pl.loop(0, 1)
        def _(t):
            for f in range(RANKS):
                ms_ref[i, f] = attended(i, f, table_ref, head).astype(jnp.bfloat16)

        for j in (2, 3, 1):
            f = pair_of(r, j)
            go(
                ms_ref.at[i, f], mix_ref.at[RANKS * i + r], msend_sem.at[i, j],
                mland_sem.at[RANKS * i + r], {"seq": RANKS * z + f},
            )
        mix_ref[RANKS * i + r] = ms_ref[i, r]

    def mixed():
        for j in range(1, RANKS):
            for i in range(RANKS):
                h = RANKS * i + pair_of(r, j)
                move(
                    ms_ref.at[0, 0], mix_ref.at[h], msend_sem.at[0, 1], mland_sem.at[h], other
                ).wait_recv()

    def project_back(phase, lanes=slice(None)):
        @pl.loop(0, RANKS)
        def _(zz):
            update = jnp.dot(
                w_ref[phase, zz, 3:7].reshape(wide, width),
                mix_ref[:, :, lanes].reshape(width, -1),
                preferred_element_type=jnp.float32,
            )
            at = pl.ds(pl.multiple_of(zz * wide, 8), wide)
            xt_ref[at, lanes] = xt_ref[at, lanes] + update

    def normalize_again(lanes=slice(None)):
        values = xt_ref[:, lanes].astype(jnp.bfloat16).astype(jnp.float32)
        xt_ref[:, lanes] = values
        centered = values - jnp.mean(values, axis=0, keepdims=True)
        spread = jnp.mean(centered * centered, axis=0, keepdims=True)
        nb_ref[lanes, :] = (centered * lax.rsqrt(spread + epsilon)).T.astype(jnp.bfloat16)


    def rows(zz, part):
        return pl.ds(pl.multiple_of((RANKS * part + zz) * count, count), count)

    def scatter(parts=range(RANKS)):
        for part in parts:
            for j in range(1, RANKS):
                to = pair_of(z, j)
                go(
                    nb_ref.at[rows(to, part)], g_ref.at[part, RANKS * r + z],
                    asend_sem.at[part, j], gz_sem.at[part, z], {"seq": RANKS * to + r},
                )
        for part in parts:
            g_ref[part, RANKS * r + z] = nb_ref[rows(z, part), :]

    def frames(part, rank, which, device):
        at = g_ref.at[part, pl.ds(RANKS * rank, RANKS)]
        return move(at, at, fsend_sem.at[part, which], gr_sem.at[part, rank], device)

    def forward(part):
        for j in range(1, RANKS):
            source = pair_of(z, j)
            move(
                nb_ref.at[rows(0, 0)], g_ref.at[part, RANKS * r + source],
                asend_sem.at[0, 1], gz_sem.at[part, source], other,
            ).wait_recv()
        frames(part, r, 1, far).start()
        frames(part, r, 0, sib).start()

    def relay(part):
        rank = pair_of(r, 2)
        frames(part, rank, 0, sib).wait_recv()
        frames(part, rank, 2, sib).start()

    def ready(part):
        for j in (1, 3):
            frames(part, pair_of(r, j), 0, sib).wait_recv()

    def temporal(part):
        out = lax.dot_general(
            w_ref[1, :, 0:3].reshape(3 * wide, width), g_ref[part].reshape(tokens, width),
            (((1,), (1,)), ((), ())), preferred_element_type=jnp.float32,
        )
        for slot in range(3 * RANKS):
            piece = out[slot * head : (slot + 1) * head]
            table_ref[slot, part, :head] = piece.astype(jnp.bfloat16)

    def temporal_heads(part):
        @pl.loop(0, 1)
        def _(t):
            for i in range(RANKS):
                at = pl.ds(pl.multiple_of(i * head, 8), head)
                mt_ref[at, :] = attended(i, part, table_ref, head, count)

        rs_ref[part] = mt_ref[...].T.astype(jnp.bfloat16).reshape(rs_ref.shape[1:])

    def back(part, j):
        to = lax.rem(me + j, n)
        zt, rt = lax.div(to, RANKS), lax.rem(to, RANKS)
        return move(
            rs_ref.at[part, RANKS * rt + zt], mr_ref.at[r, RANKS * part + z],
            rsend_sem.at[part, j], rland_sem.at[r, RANKS * part + z], {"seq": to},
        )

    half, parts = tokens // 2, RANKS // 2

    def returned(which):
        for j in range(1, n):
            source = lax.rem(me + j, n)
            zt, rt = lax.div(source, RANKS), lax.rem(source, RANKS)
            for part in range(which * parts, (which + 1) * parts):
                move(
                    rs_ref.at[0, 0], mr_ref.at[rt, RANKS * part + zt],
                    rsend_sem.at[0, 1], rland_sem.at[rt, RANKS * part + zt], other,
                ).wait_recv()
        lanes = slice(which * half, (which + 1) * half)
        taken = slice(which * n // 2, (which + 1) * n // 2)
        for rank in range(RANKS):
            turned = mr_ref[rank, taken].reshape(half, -1).astype(jnp.float32).T
            for i in range(RANKS):
                piece = turned[i * head : (i + 1) * head]
                mix_ref[RANKS * i + rank, :, lanes] = piece.astype(jnp.bfloat16)
        project_back(1, lanes)
        out_ref[lanes, :] = xt_ref[:, lanes].T.astype(jnp.bfloat16)

    barrier = pltpu.get_barrier_semaphore()
    greeted = [other, sib, far]
    for device in greeted:
        pl.semaphore_signal(barrier, inc=1, device_id=device, device_id_type=MESH)
    for inside, way in ((z < RANKS - 1, 1), (z > 0, -1)):

        @pl.when(inside)
        def _():
            device = {"seq": me + RANKS * way}
            pl.semaphore_signal(barrier, inc=1, device_id=device, device_id_type=MESH)

    copies = [pltpu.make_async_copy(x_ref, x_vmem, keep_sem.at[2, 0])]
    copies += [*keep(0, sq_ref, so_ref), *keep(1, tq_ref, to_ref)]
    for one in copies:
        one.start()
    table_ref[2 * RANKS :, :, head:, :] = jnp.ones_like(table_ref[2 * RANKS :, :, head:, :])
    mt_ref[...] = jnp.zeros_like(mt_ref)
    copies[0].wait()
    middle = (z > 0) & (z < RANKS - 1)
    pl.semaphore_wait(barrier, len(greeted) + 1 + lax.rem(lax.div(z + 1, 2), 2))

    one, two, three = (pair_of(r, j) for j in (1, 2, 3))
    near = [pair_of(z, j) for j in range(RANKS)]
    deal(0, sq_ref)
    for each in copies[1:3]:
        each.wait()
    by_pair(z, 0, lambda: along(0, 0))
    landed(0, z, sib_slot)
    by_pair(z, 1, lambda: along(0, 0))
    normalize_into(x_vmem, xt_ref, na_ref.at[r])
    share(r, 1, far)
    share(r, 0, sib)
    landed(0, z, far_slot)
    by_pair(z, 0, lambda: along(0, 1))
    deal(1, tq_ref)
    hop(0, 1, 0)
    normed(one, 0, sib).wait_recv()
    project(z, r, one)
    out_first(0, z)
    hop(0, 1, 1, 0)
    hop(0, 2, 0)
    from_twin(0, near[1], 0)
    hop(0, 3, 0)
    hop(0, 2, 1, 0)
    by_pair(z, 1, lambda: along(0, 1))
    hop(0, 1, 1, 1)
    normed(two, 0, sib).wait_recv()
    share(two, 2, sib)

    @pl.when(middle)
    def _():
        hop(0, 2, 1, 1)

    for each in copies[3:]:
        each.wait()
    landed(1, z, sib_slot)
    landed(1, z, far_slot)
    along(1, 0)
    along(1, 1)
    by_pair(near[1], 1, lambda: from_twin(0, near[1], 1))
    project(near[1], r, one)
    normed(three, 0, sib).wait_recv()
    project(z, two, three)
    project(near[1], two, three)
    from_twin(0, near[2], 0)
    by_pair(near[2], 1, lambda: from_twin(0, near[2], 1))
    project_all(near[2])
    hop(0, 3, 1, 0)

    @pl.when(jnp.logical_not(middle))
    def _():
        hop(0, 2, 1, 1)

    hop(0, 3, 1, 1)
    from_twin(0, near[3], 0)
    by_pair(near[3], 1, lambda: from_twin(0, near[3], 1))
    project_all(near[3])
    for j in (1, 2):
        by_pair(near[j], 0, lambda: out_twin(0, near[j]))
    hop(1, 1, 0)
    spatial_head(0)
    hop(1, 1, 1)
    spatial_head(1)
    by_pair(near[3], 0, lambda: out_twin(0, near[3]))
    hop(1, 2, 0)
    spatial_head(2)
    spatial_head(3)
    hop(1, 3, 0)
    out_first(1, z)
    for j in range(1, RANKS):
        by_pair(near[j], 1, lambda: out_first(1, near[j]))

    @pl.when(middle)
    def _():
        hop(1, 2, 1)

    out_relay(0)
    mixed()
    out_last(0)
    for j in range(1, RANKS):
        by_pair(near[j], 0, lambda: out_twin(1, near[j]))
    for which in range(2):
        lanes = slice(which * half, (which + 1) * half)
        project_back(0, lanes)
        normalize_again(lanes)
        scatter(range(which * parts, (which + 1) * parts))

    @pl.when(jnp.logical_not(middle))
    def _():
        hop(1, 2, 1)

    hop(1, 3, 1)
    for part in range(RANKS - 1):
        forward(part)
    relay(0)
    for j in range(1, RANKS):
        by_pair(near[j], 1, lambda: from_twin(1, near[j], 0))
        from_twin(1, near[j], 1)

    @pl.loop(0, RANKS)
    def _(part):
        ready(part)

        @pl.when(part == 0)
        def _():
            forward(RANKS - 1)

        temporal(part)

        @pl.when(part < RANKS - 1)
        def _():
            relay(part + 1)

        @pl.when(part == 1)
        def _():
            out_relay(1)

        temporal_heads(part)
        for j in range(1, n):
            back(part, j).start()
        mr_ref[r, RANKS * part + z] = rs_ref[part, RANKS * r + z]

    out_last(1)
    for which in range(2):
        returned(which)

    for one in sends:
        one.wait_send()
    for phase in range(2):
        for b in range(2):
            for zz in range(RANKS):

                @pl.when((z >= zz) & (z < RANKS - 1))
                def _():
                    line(phase, zz, b, 0).wait_send()

                @pl.when((z <= zz) & (z > 0))
                def _():
                    line(phase, zz, b, 1).wait_send()

            for j in range(1, RANKS):
                twin(phase, near[j], b).wait_send()
        for zz in range(RANKS):
            over(phase, zz).wait_send()
            beside(phase, zz, 0, r).wait_send()
            beside(phase, zz, 1, two).wait_send()

    @pl.loop(0, RANKS)
    def _(part):
        for which, rank in ((0, r), (1, r), (2, pair_of(r, 2))):
            frames(part, rank, which, sib).wait_send()
        for j in range(1, n):
            back(part, j).wait_send()


def fused(video, spatial_qkv, spatial_out, temporal_qkv, temporal_out):
    _, tokens, width = video.shape
    n = lax.axis_size("seq")
    head, count = width // HEADS, tokens // n
    padded = -(-RANKS * head // 128) * 128
    vmem, dma = pltpu.VMEM, pltpu.SemaphoreType.DMA
    half = jnp.bfloat16

    def blocks(w):
        return w.T.reshape(-1, head, width)

    out = pl.pallas_call(
        functools.partial(fused_kernel, count),
        out_shape=jax.ShapeDtypeStruct((tokens, width), half),
        in_specs=[pl.BlockSpec(memory_space=pl.ANY)] * 5,
        out_specs=pl.BlockSpec(memory_space=pltpu.VMEM),
        scratch_shapes=[
            vmem((2, RANKS, 3 + RANKS, head, width), half),
            vmem((RANKS, width, tokens), half),
            vmem((width, tokens), jnp.float32),
            vmem((3 * RANKS, RANKS, head + 8, tokens), half),
            vmem((RANKS, RANKS, head, tokens), half),
            vmem((HEADS, head, tokens), half),
            vmem((tokens, width), half),
            vmem((RANKS, n, count, width), half),
            vmem((padded, tokens), jnp.float32),
            vmem((RANKS, n, count, padded), half),
            vmem((RANKS, n, count, padded), half),
            dma((2, RANKS, 3 + RANKS)),
            dma((2, 2)),
            dma((2, 2, RANKS, 2)),
            dma((2, RANKS, 2)),
            dma((2, RANKS, 2)),
            dma((2, RANKS)),
            dma((RANKS,)),
            dma((3,)),
            dma((RANKS, RANKS)),
            dma((HEADS,)),
            dma((RANKS, RANKS)),
            dma((RANKS, RANKS)),
            dma((RANKS, 3)),
            dma((RANKS, RANKS)),
            dma((RANKS, n)),
            dma((RANKS, n)),
            vmem((tokens, width), half),
            dma((3, 2)),
        ],
        compiler_params=pltpu.CompilerParams(
            collective_id=0, has_side_effects=True, vmem_limit_bytes=60 << 20
        ),
    )(
        video.reshape(tokens, width),
        blocks(spatial_qkv), blocks(spatial_out), blocks(temporal_qkv), blocks(temporal_out),
    )
    return out.reshape(video.shape)


def local(video, spatial_qkv, *rest):
    n, groups = lax.axis_size("seq"), lax.axis_size("groups")
    frames_here, patches, _ = video.shape
    ringed = n == HEADS and groups % 2 == 0 and frames_here == 1 and patches % (16 * n) == 0
    return (fused if ringed else plain)(video, spatial_qkv, *rest)


def solution(mesh):
    split = P(None, "seq")
    placed = (P(("groups", "seq"), None, None), split, split, split, split)
    return jax.shard_map(
        local,
        mesh=mesh,
        in_specs=placed,
        out_specs=placed[0],
        check_vma=False,
    )
```

```python
import functools
import math

import jax
import jax.numpy as jnp
from jax import lax
from jax.experimental import pallas as pl
from jax.experimental.pallas import tpu as pltpu
from jax.sharding import PartitionSpec as P

HEADS = 16
epsilon = 1e-06
MESH = pl.DeviceIdType.MESH


def normalize_into(x_ref, xt_ref, nt_ref):
    xt_ref[...] = x_ref[...].astype(jnp.float32).T
    values = xt_ref[...]
    centered = values - jnp.mean(values, axis=0, keepdims=True)
    spread = jnp.mean(centered * centered, axis=0, keepdims=True)
    nt_ref[...] = (centered * lax.rsqrt(spread + epsilon)).astype(jnp.bfloat16)


def project_shard(w_ref, shard, nt_ref, table_ref):
    blocks, rows, width = w_ref.shape[1:]
    head = table_ref.shape[1]
    out = jnp.dot(
        w_ref[shard].reshape(blocks * rows, width), nt_ref[...], preferred_element_type=jnp.float32
    ).astype(jnp.bfloat16)
    for j in range(blocks):
        table_ref[shard * blocks + j] = out[j * rows : j * rows + head]


def attend_pair(pair, table_ref, mixed_ref, same, low=0, high=None):
    head = table_ref.shape[1]
    parts = []
    for j in range(2):
        h = pair * 2 + j
        q, k, v = table_ref[h, :, low:high], table_ref[HEADS + h], table_ref[2 * HEADS + h]
        scores = lax.dot_general(
            k, q, (((0,), (0,)), ((), ())), preferred_element_type=jnp.float32
        ) * (1.0 / math.sqrt(head))
        if same is not None:
            scores = jnp.where(same(scores.shape), scores, -jnp.inf)
        powers = jnp.exp(scores - jnp.max(scores, axis=0, keepdims=True))
        total = jnp.sum(powers, axis=0, keepdims=True)
        probs = (powers * (1.0 / total)).astype(jnp.bfloat16)
        parts.append(jnp.dot(v, probs, preferred_element_type=jnp.float32))
    both = jnp.concatenate(parts, axis=0).astype(jnp.bfloat16)
    mixed_ref[pl.ds(pl.multiple_of(pair * 2 * head, 16), 2 * head), low:high] = both


def project_out(w_ref, mixed_ref, xt_ref, out_ref, head, first=0, last=None):
    shards, blocks, rows, width = w_ref.shape
    low = head // 16 * 16
    step = 4
    tokens = slice(first, last)

    @pl.loop(0, shards // step)
    def _(i):
        weights = w_ref[pl.ds(i * step, step), :, low:, :].reshape(-1, width)
        update = jnp.dot(weights, mixed_ref[:, tokens], preferred_element_type=jnp.float32)
        update = update.reshape(step * blocks, rows - low, -1)[:, head - low :]
        count = step * blocks * (rows - head)
        at = pl.ds(pl.multiple_of(i * count, 8), count)
        xt_ref[at, tokens] = xt_ref[at, tokens] + update.reshape(count, -1)

    out_ref[tokens, :] = xt_ref[:, tokens].T.astype(jnp.bfloat16)


def same_by(kind, size):
    def same(shape):
        a = lax.broadcasted_iota(jnp.int32, shape, 0)
        b = lax.broadcasted_iota(jnp.int32, shape, 1)
        return (a % size == b % size) if kind == "mod" else (a // size == b // size)

    return same


def sublayer_kernel(same, x_ref, w_ref, out_ref, xt_ref, nt_ref, table_ref, mixed_ref):
    normalize_into(x_ref, xt_ref, nt_ref)

    @pl.loop(0, w_ref.shape[0])
    def _(d):
        project_shard(w_ref, d, nt_ref, table_ref)

    @pl.loop(0, HEADS // 2)
    def _(pair):
        attend_pair(pair, table_ref, mixed_ref, same)

    project_out(w_ref, mixed_ref, xt_ref, out_ref, table_ref.shape[1])


def compute_scratch(tokens, width):
    return [
        pltpu.VMEM((width, tokens), jnp.float32),
        pltpu.VMEM((width, tokens), jnp.bfloat16),
        pltpu.VMEM((3 * HEADS, width // HEADS, tokens), jnp.bfloat16),
        pltpu.VMEM((width, tokens), jnp.bfloat16),
    ]


def sublayer(x, w, same):
    tokens, width = x.shape
    return pl.pallas_call(
        functools.partial(sublayer_kernel, same),
        out_shape=jax.ShapeDtypeStruct(x.shape, jnp.bfloat16),
        in_specs=[pl.BlockSpec(memory_space=pltpu.VMEM)] * 2,
        out_specs=pl.BlockSpec(memory_space=pltpu.VMEM),
        scratch_shapes=compute_scratch(tokens, width),
        compiler_params=pltpu.CompilerParams(vmem_limit_bytes=40 << 20),
    )(x, w)


def blocks_of(qkv, out, count):
    width = qkv.shape[0]
    return jnp.concatenate(
        [qkv.T.reshape(count, -1, width), out.T.reshape(count, -1, width)], axis=1
    )


def gathered(qkv, out):
    if lax.axis_size("seq") == HEADS:
        return lax.all_gather(blocks_of(qkv, out, 3), "seq", axis=0)
    full = blocks_of(
        lax.all_gather(qkv, "seq", axis=1, tiled=True),
        lax.all_gather(out, "seq", axis=1, tiled=True),
        3 * HEADS,
    )
    return full.reshape(HEADS, 3, *full.shape[1:])


def plain(video, spatial_qkv, spatial_out, temporal_qkv, temporal_out):
    frames_here, patches, width = video.shape
    n = lax.axis_size("seq")
    count = patches // n
    same_s = None if frames_here == 1 else same_by("div", patches)
    hidden = sublayer(video.reshape(-1, width), gathered(spatial_qkv, spatial_out), same_s)
    blocks = hidden.reshape(frames_here, n, count, width)
    received = lax.all_to_all(blocks, "seq", split_axis=1, concat_axis=0, tiled=True)
    result = sublayer(
        received.reshape(-1, width), gathered(temporal_qkv, temporal_out), same_by("mod", count)
    )
    positioned = result.reshape(frames_here * n, 1, count, width)
    returned = lax.all_to_all(positioned, "seq", split_axis=0, concat_axis=1, tiled=True)
    return returned.reshape(frames_here, patches, width)


RANKS = 4


def pair_of(value, j):
    if j == 0:
        return value
    if j == 1:
        return value + 1 - 2 * lax.rem(value, 2)
    if j == 2:
        return lax.rem(value + 2, 4)
    return 3 - value


def attended(i, at, table_ref, head, period=None):
    heads = table_ref.shape[0] // 3
    q, k = table_ref[i, at, :head], table_ref[heads + i, at, :head]
    v = table_ref[2 * heads + i, at]
    scores = lax.dot_general(k, q, (((0,), (0,)), ((), ())), preferred_element_type=jnp.float32)
    if period is not None:
        keys, queries = scores.shape
        a = lax.broadcasted_iota(jnp.int32, (1, period, queries), 1)
        b = lax.broadcasted_iota(jnp.int32, (1, period, queries), 2)
        parts = scores.reshape(keys // period, period, queries)
        scores = jnp.where(a == b % period, parts, -jnp.inf).reshape(keys, queries)
    centered = scores - jnp.max(scores, axis=0, keepdims=True)
    powers = jnp.exp2(centered * (math.log2(math.e) / math.sqrt(head))).astype(jnp.bfloat16)
    out = jnp.dot(v, powers, preferred_element_type=jnp.float32)
    return out[:head] * (1.0 / out[head : head + 1])


def fused_kernel(
    count, x_ref, sq_ref, so_ref, tq_ref, to_ref, out_ref,
    w_ref, na_ref, xt_ref, table_ref, ms_ref, mix_ref, nb_ref, g_ref, mt_ref, rs_ref, mr_ref,
    land_sem, deal_sem, line_sem, twin_sem, osib_sem, oy_sem, ox_sem, nland_sem, nsend_sem,
    msend_sem, mland_sem, asend_sem, gz_sem, fsend_sem, gr_sem, rsend_sem, rland_sem,
    x_vmem, keep_sem,
):
    n = HEADS
    me = lax.axis_index("seq")
    group = lax.axis_index("groups")
    z, r = lax.div(me, RANKS), lax.rem(me, RANKS)
    core, row = lax.rem(r, 2), lax.div(r, 2)
    side = lax.rem(group, 2)
    other = {"groups": group + 1 - 2 * side}
    sib = {"seq": RANKS * z + pair_of(r, 1)}
    far = {"seq": RANKS * z + pair_of(r, 2)}
    head = mix_ref.shape[1]
    width, tokens = xt_ref.shape
    wide = RANKS * head

    def move(src, dst, send, recv, device):
        return pltpu.make_async_remote_copy(
            src_ref=src, dst_ref=dst, send_sem=send, recv_sem=recv,
            device_id=device, device_id_type=MESH,
        )

    sends = []

    def go(*what):
        one = move(*what)
        one.start()
        sends.append(one)


    own_slot = lax.div(3 * r + 2 * core, RANKS)
    sib_slot = lax.div(3 * pair_of(r, 1) + 1, RANKS)
    far_slot = 2 - 2 * row

    def slot_of(phase, pair, b):
        if b == 0:
            return (1 - pair) * own_slot + pair * ((3 + r) if phase else sib_slot)
        return (1 - pair) * far_slot + pair * (sib_slot if phase else (3 + r))

    def mine(phase, zz, b):
        return slot_of(phase, lax.rem(zz + side, 2), b)

    def theirs(phase, zz, b):
        return slot_of(phase, 1 - lax.rem(zz + side, 2), b)

    def block(phase, zz, slot, send, device):
        at = w_ref.at[phase, zz, slot]
        return move(at, at, send, land_sem.at[phase, zz, slot], device)

    def landed(phase, zz, slot):
        block(phase, zz, slot, deal_sem.at[0, 0], other).wait_recv()

    def line(phase, zz, b, way):
        device = {"seq": me + RANKS * (1 - 2 * way)}
        return block(phase, zz, mine(phase, zz, b), line_sem.at[phase, way, zz, b], device)

    def twin(phase, zz, b):
        return block(phase, zz, mine(phase, zz, b), twin_sem.at[phase, zz, b], other)

    def keep(phase, q_ref, o_ref):
        return (
            pltpu.make_async_copy(q_ref.at[2 * core], w_ref.at[phase, z, own_slot], keep_sem.at[phase, 0]),
            pltpu.make_async_copy(o_ref.at[0], w_ref.at[phase, z, 3 + r], keep_sem.at[phase, 1]),
        )

    def deal(phase, q_ref):
        for which, j, device in ((0, 2 - 2 * core, far), (1, 1, sib)):
            slot = lax.div(3 * r + j, RANKS)
            go(
                q_ref.at[j], w_ref.at[phase, z, slot], deal_sem.at[phase, which],
                land_sem.at[phase, z, slot], device,
            )

    def along(phase, b):
        @pl.when(z < RANKS - 1)
        def _():
            line(phase, z, b, 0).start()

        @pl.when(z > 0)
        def _():
            line(phase, z, b, 1).start()

    def by_pair(zz, pair, run):
        @pl.when(lax.rem(zz + side, 2) == pair)
        def _():
            run()

    def onward(phase, zz, b):
        twin(phase, zz, b).start()
        if phase == 0 and b == 1:

            @pl.when(lax.rem(zz + side, 2) == 1)
            def _():
                out_first(phase, zz)

    def hop(phase, d, b, pair=None):
        def wanted(zz):
            return True if pair is None else lax.rem(zz + side, 2) == pair

        @pl.when((z >= d) & wanted(z + RANKS - d))
        def _():
            landed(phase, z - d, mine(phase, z - d, b))

            @pl.when(z < RANKS - 1)
            def _():
                line(phase, z - d, b, 0).start()

            onward(phase, z - d, b)

        @pl.when((z + d < RANKS) & wanted(z + d))
        def _():
            landed(phase, z + d, mine(phase, z + d, b))

            @pl.when(z > 0)
            def _():
                line(phase, z + d, b, 1).start()

            onward(phase, z + d, b)

    def from_twin(phase, zz, *which):
        for b in which:
            landed(phase, zz, theirs(phase, zz, b))


    def beside(phase, zz, which, rank):
        return block(phase, zz, 3 + rank, osib_sem.at[phase, zz, which], sib)

    def over(phase, zz):
        return block(phase, zz, 3 + r, oy_sem.at[phase, zz], far)

    def out_first(phase, zz):
        over(phase, zz).start()
        beside(phase, zz, 0, r).start()

    def out_twin(phase, zz):
        from_twin(phase, zz, 1 - phase)
        if phase == 0:
            out_first(phase, zz)
        else:
            beside(phase, zz, 0, r).start()


    def out_across(k):
        zz, rank = 2 * k + 1 - side, pair_of(r, 2)
        return block(1, zz, 3 + rank, ox_sem.at[k], other)

    def out_second(k):
        zz, rank = 2 * k + 1 - side, pair_of(r, 2)
        landed(1, zz, 3 + rank)
        out_across(k).start()
        beside(1, zz, 1, rank).start()

    def out_third(k):
        zz, rank = 2 * k + side, pair_of(r, 2)
        landed(1, zz, 3 + rank)
        beside(1, zz, 1, rank).start()

    def out_relay(phase):
        for zz in range(RANKS):
            landed(phase, zz, 3 + pair_of(r, 2))
            beside(phase, zz, 1, pair_of(r, 2)).start()

    def out_last(phase):
        for zz in range(RANKS):
            landed(phase, zz, 3 + pair_of(r, 1))
            landed(phase, zz, 3 + pair_of(r, 3))


    def normed(f, which, device):
        at = na_ref.at[f]
        return move(at, at, nsend_sem.at[which], nland_sem.at[f], device)

    def share(f, which, device):
        one = normed(f, which, device)
        one.start()
        sends.append(one)

    def project(zz, *frames):
        for f in frames:
            out = jnp.dot(
                w_ref[0, zz, 0:3].reshape(3 * head, width), na_ref[f],
                preferred_element_type=jnp.float32,
            )
            for slot in range(3):
                piece = out[slot * head : (slot + 1) * head]
                table_ref[3 * zz + slot, f, :head] = piece.astype(jnp.bfloat16)

    def project_all(zz):
        @pl.loop(0, RANKS)
        def _(f):
            project(zz, f)

    def spatial_head(i):
        @pl.loop(0, 1)
        def _(t):
            for f in range(RANKS):
                ms_ref[i, f] = attended(i, f, table_ref, head).astype(jnp.bfloat16)

        for j in (2, 3, 1):
            f = pair_of(r, j)
            go(
                ms_ref.at[i, f], mix_ref.at[RANKS * i + r], msend_sem.at[i, j],
                mland_sem.at[RANKS * i + r], {"seq": RANKS * z + f},
            )
        mix_ref[RANKS * i + r] = ms_ref[i, r]

    def mixed():
        for j in range(1, RANKS):
            for i in range(RANKS):
                h = RANKS * i + pair_of(r, j)
                move(
                    ms_ref.at[0, 0], mix_ref.at[h], msend_sem.at[0, 1], mland_sem.at[h], other
                ).wait_recv()

    def project_back(phase, lanes=slice(None)):
        @pl.loop(0, RANKS)
        def _(zz):
            update = jnp.dot(
                w_ref[phase, zz, 3:7].reshape(wide, width),
                mix_ref[:, :, lanes].reshape(width, -1),
                preferred_element_type=jnp.float32,
            )
            at = pl.ds(pl.multiple_of(zz * wide, 8), wide)
            xt_ref[at, lanes] = xt_ref[at, lanes] + update

    def normalize_again(lanes=slice(None)):
        values = xt_ref[:, lanes].astype(jnp.bfloat16).astype(jnp.float32)
        xt_ref[:, lanes] = values
        centered = values - jnp.mean(values, axis=0, keepdims=True)
        spread = jnp.mean(centered * centered, axis=0, keepdims=True)
        nb_ref[lanes, :] = (centered * lax.rsqrt(spread + epsilon)).T.astype(jnp.bfloat16)


    def rows(zz, part):
        return pl.ds(pl.multiple_of((RANKS * part + zz) * count, count), count)

    def scatter(parts=range(RANKS)):
        for part in parts:
            for j in range(1, RANKS):
                to = pair_of(z, j)
                go(
                    nb_ref.at[rows(to, part)], g_ref.at[part, RANKS * r + z],
                    asend_sem.at[part, j], gz_sem.at[part, z], {"seq": RANKS * to + r},
                )
        for part in parts:
            g_ref[part, RANKS * r + z] = nb_ref[rows(z, part), :]

    def frames(part, rank, which, device):
        at = g_ref.at[part, pl.ds(RANKS * rank, RANKS)]
        return move(at, at, fsend_sem.at[part, which], gr_sem.at[part, rank], device)

    def forward(part):
        for j in range(1, RANKS):
            source = pair_of(z, j)
            move(
                nb_ref.at[rows(0, 0)], g_ref.at[part, RANKS * r + source],
                asend_sem.at[0, 1], gz_sem.at[part, source], other,
            ).wait_recv()
        frames(part, r, 1, far).start()
        frames(part, r, 0, sib).start()

    def relay(part):
        rank = pair_of(r, 2)
        frames(part, rank, 0, sib).wait_recv()
        frames(part, rank, 2, sib).start()

    def ready(part):
        for j in (1, 3):
            frames(part, pair_of(r, j), 0, sib).wait_recv()

    def temporal(part):
        out = lax.dot_general(
            w_ref[1, :, 0:3].reshape(3 * wide, width), g_ref[part].reshape(tokens, width),
            (((1,), (1,)), ((), ())), preferred_element_type=jnp.float32,
        )
        for slot in range(3 * RANKS):
            piece = out[slot * head : (slot + 1) * head]
            table_ref[slot, part, :head] = piece.astype(jnp.bfloat16)

    def temporal_heads(part):
        @pl.loop(0, 1)
        def _(t):
            for i in range(RANKS):
                at = pl.ds(pl.multiple_of(i * head, 8), head)
                mt_ref[at, :] = attended(i, part, table_ref, head, count)

        rs_ref[part] = mt_ref[...].T.astype(jnp.bfloat16).reshape(rs_ref.shape[1:])

    def back(part, j):
        to = lax.rem(me + j, n)
        zt, rt = lax.div(to, RANKS), lax.rem(to, RANKS)
        return move(
            rs_ref.at[part, RANKS * rt + zt], mr_ref.at[r, RANKS * part + z],
            rsend_sem.at[part, j], rland_sem.at[r, RANKS * part + z], {"seq": to},
        )

    half, parts = tokens // 2, RANKS // 2

    def returned(which):
        for j in range(1, n):
            source = lax.rem(me + j, n)
            zt, rt = lax.div(source, RANKS), lax.rem(source, RANKS)
            for part in range(which * parts, (which + 1) * parts):
                move(
                    rs_ref.at[0, 0], mr_ref.at[rt, RANKS * part + zt],
                    rsend_sem.at[0, 1], rland_sem.at[rt, RANKS * part + zt], other,
                ).wait_recv()
        lanes = slice(which * half, (which + 1) * half)
        taken = slice(which * n // 2, (which + 1) * n // 2)
        for rank in range(RANKS):
            turned = mr_ref[rank, taken].reshape(half, -1).astype(jnp.float32).T
            for i in range(RANKS):
                piece = turned[i * head : (i + 1) * head]
                mix_ref[RANKS * i + rank, :, lanes] = piece.astype(jnp.bfloat16)
        project_back(1, lanes)
        out_ref[lanes, :] = xt_ref[:, lanes].T.astype(jnp.bfloat16)

    barrier = pltpu.get_barrier_semaphore()
    greeted = [other, sib, far]
    for device in greeted:
        pl.semaphore_signal(barrier, inc=1, device_id=device, device_id_type=MESH)
    for inside, way in ((z < RANKS - 1, 1), (z > 0, -1)):

        @pl.when(inside)
        def _():
            device = {"seq": me + RANKS * way}
            pl.semaphore_signal(barrier, inc=1, device_id=device, device_id_type=MESH)

    copies = [pltpu.make_async_copy(x_ref, x_vmem, keep_sem.at[2, 0])]
    copies += [*keep(0, sq_ref, so_ref), *keep(1, tq_ref, to_ref)]
    for one in copies:
        one.start()
    table_ref[2 * RANKS :, :, head:, :] = jnp.ones_like(table_ref[2 * RANKS :, :, head:, :])
    mt_ref[...] = jnp.zeros_like(mt_ref)
    copies[0].wait()
    middle = (z > 0) & (z < RANKS - 1)
    pl.semaphore_wait(barrier, len(greeted) + 1 + lax.rem(lax.div(z + 1, 2), 2))

    one, two, three = (pair_of(r, j) for j in (1, 2, 3))
    near = [pair_of(z, j) for j in range(RANKS)]
    deal(0, sq_ref)
    for each in copies[1:3]:
        each.wait()
    by_pair(z, 0, lambda: along(0, 0))
    for each in copies[3:]:
        each.wait()
    by_pair(z, 1, lambda: along(1, 0))
    landed(0, z, sib_slot)
    by_pair(z, 1, lambda: along(0, 0))
    normalize_into(x_vmem, xt_ref, na_ref.at[r])
    deal(1, tq_ref)
    share(r, 1, far)
    share(r, 0, sib)
    landed(0, z, far_slot)
    by_pair(z, 0, lambda: along(0, 1))
    hop(0, 1, 0)
    normed(one, 0, sib).wait_recv()
    project(z, r, one)
    out_first(0, z)
    hop(0, 1, 1, 0)
    hop(0, 2, 0)
    from_twin(0, near[1], 0)
    hop(0, 3, 0)
    hop(0, 2, 1, 0)
    by_pair(z, 1, lambda: along(0, 1))
    hop(0, 1, 1, 1)
    normed(two, 0, sib).wait_recv()
    share(two, 2, sib)

    @pl.when(middle)
    def _():
        hop(0, 2, 1, 1)

    landed(1, z, sib_slot)
    landed(1, z, far_slot)
    by_pair(z, 0, lambda: along(1, 0))
    along(1, 1)
    by_pair(near[1], 1, lambda: from_twin(0, near[1], 1))
    project(near[1], r, one)
    normed(three, 0, sib).wait_recv()
    project(z, two, three)
    project(near[1], two, three)
    from_twin(0, near[2], 0)
    by_pair(near[2], 1, lambda: from_twin(0, near[2], 1))
    project_all(near[2])
    hop(0, 3, 1, 0)

    @pl.when(jnp.logical_not(middle))
    def _():
        hop(0, 2, 1, 1)

    hop(0, 3, 1, 1)
    from_twin(0, near[3], 0)
    by_pair(near[3], 1, lambda: from_twin(0, near[3], 1))
    project_all(near[3])
    for j in (1, 2):
        by_pair(near[j], 0, lambda: out_twin(0, near[j]))
    hop(1, 1, 0)
    spatial_head(0)
    hop(1, 1, 1)
    spatial_head(1)
    by_pair(near[3], 0, lambda: out_twin(0, near[3]))
    hop(1, 2, 0)
    spatial_head(2)
    spatial_head(3)
    hop(1, 3, 0)
    by_pair(z, 1, lambda: out_first(1, z))
    by_pair(z, 0, lambda: beside(1, z, 0, r).start())
    for j in range(1, RANKS):
        by_pair(near[j], 1, lambda: out_first(1, near[j]))

    @pl.when(middle)
    def _():
        hop(1, 2, 1)

    out_relay(0)
    mixed()

    @pl.when(jnp.logical_not(middle))
    def _():
        hop(1, 2, 1)

    out_last(0)
    for j in range(1, RANKS):
        by_pair(near[j], 0, lambda: out_twin(1, near[j]))
    for which in range(2):
        lanes = slice(which * half, (which + 1) * half)
        project_back(0, lanes)
        normalize_again(lanes)
        scatter(range(which * parts, (which + 1) * parts))

    hop(1, 3, 1)
    for part in range(RANKS - 1):
        forward(part)
    relay(0)
    for k in range(2):
        out_second(k)
    for j in range(1, RANKS):
        by_pair(near[j], 1, lambda: from_twin(1, near[j], 0))
        from_twin(1, near[j], 1)

    @pl.loop(0, RANKS)
    def _(part):
        ready(part)

        @pl.when(part == 0)
        def _():
            forward(RANKS - 1)

        temporal(part)

        @pl.when(part < RANKS - 1)
        def _():
            relay(part + 1)

        @pl.when(part == RANKS - 1)
        def _():
            for k in range(2):
                out_third(k)

        temporal_heads(part)
        for j in range(1, n):
            back(part, j).start()
        mr_ref[r, RANKS * part + z] = rs_ref[part, RANKS * r + z]

    out_last(1)
    for which in range(2):
        returned(which)

    for one in sends:
        one.wait_send()
    for phase in range(2):
        for b in range(2):
            for zz in range(RANKS):

                @pl.when((z >= zz) & (z < RANKS - 1))
                def _():
                    line(phase, zz, b, 0).wait_send()

                @pl.when((z <= zz) & (z > 0))
                def _():
                    line(phase, zz, b, 1).wait_send()

            for j in range(1, RANKS):
                twin(phase, near[j], b).wait_send()
        for zz in range(RANKS):
            if phase == 0:
                over(phase, zz).wait_send()
            else:
                by_pair(zz, 1, lambda: over(phase, zz).wait_send())
            beside(phase, zz, 0, r).wait_send()
            beside(phase, zz, 1, two).wait_send()

    for k in range(2):
        out_across(k).wait_send()

    @pl.loop(0, RANKS)
    def _(part):
        for which, rank in ((0, r), (1, r), (2, pair_of(r, 2))):
            frames(part, rank, which, sib).wait_send()
        for j in range(1, n):
            back(part, j).wait_send()


def fused(video, spatial_qkv, spatial_out, temporal_qkv, temporal_out):
    _, tokens, width = video.shape
    n = lax.axis_size("seq")
    head, count = width // HEADS, tokens // n
    padded = -(-RANKS * head // 128) * 128
    vmem, dma = pltpu.VMEM, pltpu.SemaphoreType.DMA
    half = jnp.bfloat16

    def blocks(w):
        return w.T.reshape(-1, head, width)

    out = pl.pallas_call(
        functools.partial(fused_kernel, count),
        out_shape=jax.ShapeDtypeStruct((tokens, width), half),
        in_specs=[pl.BlockSpec(memory_space=pl.ANY)] * 5,
        out_specs=pl.BlockSpec(memory_space=pltpu.VMEM),
        scratch_shapes=[
            vmem((2, RANKS, 3 + RANKS, head, width), half),
            vmem((RANKS, width, tokens), half),
            vmem((width, tokens), jnp.float32),
            vmem((3 * RANKS, RANKS, head + 8, tokens), half),
            vmem((RANKS, RANKS, head, tokens), half),
            vmem((HEADS, head, tokens), half),
            vmem((tokens, width), half),
            vmem((RANKS, n, count, width), half),
            vmem((padded, tokens), jnp.float32),
            vmem((RANKS, n, count, padded), half),
            vmem((RANKS, n, count, padded), half),
            dma((2, RANKS, 3 + RANKS)),
            dma((2, 2)),
            dma((2, 2, RANKS, 2)),
            dma((2, RANKS, 2)),
            dma((2, RANKS, 2)),
            dma((2, RANKS)),
            dma((2,)),
            dma((RANKS,)),
            dma((3,)),
            dma((RANKS, RANKS)),
            dma((HEADS,)),
            dma((RANKS, RANKS)),
            dma((RANKS, RANKS)),
            dma((RANKS, 3)),
            dma((RANKS, RANKS)),
            dma((RANKS, n)),
            dma((RANKS, n)),
            vmem((tokens, width), half),
            dma((3, 2)),
        ],
        compiler_params=pltpu.CompilerParams(
            collective_id=0, has_side_effects=True, vmem_limit_bytes=60 << 20
        ),
    )(
        video.reshape(tokens, width),
        blocks(spatial_qkv), blocks(spatial_out), blocks(temporal_qkv), blocks(temporal_out),
    )
    return out.reshape(video.shape)


def local(video, spatial_qkv, *rest):
    n, groups = lax.axis_size("seq"), lax.axis_size("groups")
    frames_here, patches, _ = video.shape
    ringed = n == HEADS and groups % 2 == 0 and frames_here == 1 and patches % (16 * n) == 0
    return (fused if ringed else plain)(video, spatial_qkv, *rest)


def solution(mesh):
    split = P(None, "seq")
    placed = (P(("groups", "seq"), None, None), split, split, split, split)
    return jax.shard_map(
        local,
        mesh=mesh,
        in_specs=placed,
        out_specs=placed[0],
        check_vma=False,
    )
```

```python
import functools
import math

import jax
import jax.numpy as jnp
from jax import lax
from jax.experimental import pallas as pl
from jax.experimental.pallas import tpu as pltpu
from jax.sharding import PartitionSpec as P

HEADS = 16
epsilon = 1e-06
MESH = pl.DeviceIdType.MESH


def normalize_into(x_ref, xt_ref, nt_ref):
    xt_ref[...] = x_ref[...].astype(jnp.float32).T
    values = xt_ref[...]
    centered = values - jnp.mean(values, axis=0, keepdims=True)
    spread = jnp.mean(centered * centered, axis=0, keepdims=True)
    nt_ref[...] = (centered * lax.rsqrt(spread + epsilon)).astype(jnp.bfloat16)


def project_shard(w_ref, shard, nt_ref, table_ref):
    blocks, rows, width = w_ref.shape[1:]
    head = table_ref.shape[1]
    out = jnp.dot(
        w_ref[shard].reshape(blocks * rows, width), nt_ref[...], preferred_element_type=jnp.float32
    ).astype(jnp.bfloat16)
    for j in range(blocks):
        table_ref[shard * blocks + j] = out[j * rows : j * rows + head]


def attend_pair(pair, table_ref, mixed_ref, same, low=0, high=None):
    head = table_ref.shape[1]
    parts = []
    for j in range(2):
        h = pair * 2 + j
        q, k, v = table_ref[h, :, low:high], table_ref[HEADS + h], table_ref[2 * HEADS + h]
        scores = lax.dot_general(
            k, q, (((0,), (0,)), ((), ())), preferred_element_type=jnp.float32
        ) * (1.0 / math.sqrt(head))
        if same is not None:
            scores = jnp.where(same(scores.shape), scores, -jnp.inf)
        powers = jnp.exp(scores - jnp.max(scores, axis=0, keepdims=True))
        total = jnp.sum(powers, axis=0, keepdims=True)
        probs = (powers * (1.0 / total)).astype(jnp.bfloat16)
        parts.append(jnp.dot(v, probs, preferred_element_type=jnp.float32))
    both = jnp.concatenate(parts, axis=0).astype(jnp.bfloat16)
    mixed_ref[pl.ds(pl.multiple_of(pair * 2 * head, 16), 2 * head), low:high] = both


def project_out(w_ref, mixed_ref, xt_ref, out_ref, head, first=0, last=None):
    shards, blocks, rows, width = w_ref.shape
    low = head // 16 * 16
    step = 4
    tokens = slice(first, last)

    @pl.loop(0, shards // step)
    def _(i):
        weights = w_ref[pl.ds(i * step, step), :, low:, :].reshape(-1, width)
        update = jnp.dot(weights, mixed_ref[:, tokens], preferred_element_type=jnp.float32)
        update = update.reshape(step * blocks, rows - low, -1)[:, head - low :]
        count = step * blocks * (rows - head)
        at = pl.ds(pl.multiple_of(i * count, 8), count)
        xt_ref[at, tokens] = xt_ref[at, tokens] + update.reshape(count, -1)

    out_ref[tokens, :] = xt_ref[:, tokens].T.astype(jnp.bfloat16)


def same_by(kind, size):
    def same(shape):
        a = lax.broadcasted_iota(jnp.int32, shape, 0)
        b = lax.broadcasted_iota(jnp.int32, shape, 1)
        return (a % size == b % size) if kind == "mod" else (a // size == b // size)

    return same


def sublayer_kernel(same, x_ref, w_ref, out_ref, xt_ref, nt_ref, table_ref, mixed_ref):
    normalize_into(x_ref, xt_ref, nt_ref)

    @pl.loop(0, w_ref.shape[0])
    def _(d):
        project_shard(w_ref, d, nt_ref, table_ref)

    @pl.loop(0, HEADS // 2)
    def _(pair):
        attend_pair(pair, table_ref, mixed_ref, same)

    project_out(w_ref, mixed_ref, xt_ref, out_ref, table_ref.shape[1])


def compute_scratch(tokens, width):
    return [
        pltpu.VMEM((width, tokens), jnp.float32),
        pltpu.VMEM((width, tokens), jnp.bfloat16),
        pltpu.VMEM((3 * HEADS, width // HEADS, tokens), jnp.bfloat16),
        pltpu.VMEM((width, tokens), jnp.bfloat16),
    ]


def sublayer(x, w, same):
    tokens, width = x.shape
    return pl.pallas_call(
        functools.partial(sublayer_kernel, same),
        out_shape=jax.ShapeDtypeStruct(x.shape, jnp.bfloat16),
        in_specs=[pl.BlockSpec(memory_space=pltpu.VMEM)] * 2,
        out_specs=pl.BlockSpec(memory_space=pltpu.VMEM),
        scratch_shapes=compute_scratch(tokens, width),
        compiler_params=pltpu.CompilerParams(vmem_limit_bytes=40 << 20),
    )(x, w)


def blocks_of(qkv, out, count):
    width = qkv.shape[0]
    return jnp.concatenate(
        [qkv.T.reshape(count, -1, width), out.T.reshape(count, -1, width)], axis=1
    )


def gathered(qkv, out):
    if lax.axis_size("seq") == HEADS:
        return lax.all_gather(blocks_of(qkv, out, 3), "seq", axis=0)
    full = blocks_of(
        lax.all_gather(qkv, "seq", axis=1, tiled=True),
        lax.all_gather(out, "seq", axis=1, tiled=True),
        3 * HEADS,
    )
    return full.reshape(HEADS, 3, *full.shape[1:])


def plain(video, spatial_qkv, spatial_out, temporal_qkv, temporal_out):
    frames_here, patches, width = video.shape
    n = lax.axis_size("seq")
    count = patches // n
    same_s = None if frames_here == 1 else same_by("div", patches)
    hidden = sublayer(video.reshape(-1, width), gathered(spatial_qkv, spatial_out), same_s)
    blocks = hidden.reshape(frames_here, n, count, width)
    received = lax.all_to_all(blocks, "seq", split_axis=1, concat_axis=0, tiled=True)
    result = sublayer(
        received.reshape(-1, width), gathered(temporal_qkv, temporal_out), same_by("mod", count)
    )
    positioned = result.reshape(frames_here * n, 1, count, width)
    returned = lax.all_to_all(positioned, "seq", split_axis=0, concat_axis=1, tiled=True)
    return returned.reshape(frames_here, patches, width)


RANKS = 4


def pair_of(value, j):
    if j == 0:
        return value
    if j == 1:
        return value + 1 - 2 * lax.rem(value, 2)
    if j == 2:
        return lax.rem(value + 2, 4)
    return 3 - value


def attended(i, at, table_ref, head, period=None):
    heads = table_ref.shape[0] // 3
    q, k = table_ref[i, at, :head], table_ref[heads + i, at, :head]
    v = table_ref[2 * heads + i, at]
    scores = lax.dot_general(k, q, (((0,), (0,)), ((), ())), preferred_element_type=jnp.float32)
    if period is not None:
        keys, queries = scores.shape
        a = lax.broadcasted_iota(jnp.int32, (1, period, queries), 1)
        b = lax.broadcasted_iota(jnp.int32, (1, period, queries), 2)
        parts = scores.reshape(keys // period, period, queries)
        scores = jnp.where(a == b % period, parts, -jnp.inf).reshape(keys, queries)
    centered = scores - jnp.max(scores, axis=0, keepdims=True)
    powers = jnp.exp2(centered * (math.log2(math.e) / math.sqrt(head))).astype(jnp.bfloat16)
    out = jnp.dot(v, powers, preferred_element_type=jnp.float32)
    return out[:head] * (1.0 / out[head : head + 1])


def fused_kernel(
    count, x_ref, sq_ref, so_ref, tq_ref, to_ref, out_ref,
    w_ref, na_ref, xt_ref, table_ref, ms_ref, mix_ref, nb_ref, g_ref, mt_ref, rs_ref, mr_ref,
    land_sem, deal_sem, line_sem, twin_sem, osib_sem, oy_sem, ox_sem, nland_sem, nsend_sem,
    msend_sem, mland_sem, asend_sem, gz_sem, fsend_sem, gr_sem, rsend_sem, rland_sem,
    x_vmem, keep_sem,
):
    n = HEADS
    me = lax.axis_index("seq")
    group = lax.axis_index("groups")
    z, r = lax.div(me, RANKS), lax.rem(me, RANKS)
    core, row = lax.rem(r, 2), lax.div(r, 2)
    side = lax.rem(group, 2)
    other = {"groups": group + 1 - 2 * side}
    sib = {"seq": RANKS * z + pair_of(r, 1)}
    far = {"seq": RANKS * z + pair_of(r, 2)}
    head = mix_ref.shape[1]
    width, tokens = xt_ref.shape
    wide = RANKS * head

    def move(src, dst, send, recv, device):
        return pltpu.make_async_remote_copy(
            src_ref=src, dst_ref=dst, send_sem=send, recv_sem=recv,
            device_id=device, device_id_type=MESH,
        )

    sends = []

    def go(*what):
        one = move(*what)
        one.start()
        sends.append(one)


    own_slot = lax.div(3 * r + 2 * core, RANKS)
    sib_slot = lax.div(3 * pair_of(r, 1) + 1, RANKS)
    far_slot = 2 - 2 * row

    def slot_of(phase, pair, b):
        if b == 0:
            return (1 - pair) * own_slot + pair * ((3 + r) if phase else sib_slot)
        return (1 - pair) * far_slot + pair * (sib_slot if phase else (3 + r))

    def mine(phase, zz, b):
        return slot_of(phase, lax.rem(zz + side, 2), b)

    def theirs(phase, zz, b):
        return slot_of(phase, 1 - lax.rem(zz + side, 2), b)

    def block(phase, zz, slot, send, device):
        at = w_ref.at[phase, zz, slot]
        return move(at, at, send, land_sem.at[phase, zz, slot], device)

    def landed(phase, zz, slot):
        block(phase, zz, slot, deal_sem.at[0, 0], other).wait_recv()

    def line(phase, zz, b, way):
        device = {"seq": me + RANKS * (1 - 2 * way)}
        return block(phase, zz, mine(phase, zz, b), line_sem.at[phase, way, zz, b], device)

    def twin(phase, zz, b):
        return block(phase, zz, mine(phase, zz, b), twin_sem.at[phase, zz, b], other)

    def keep(phase, q_ref, o_ref):
        return (
            pltpu.make_async_copy(q_ref.at[2 * core], w_ref.at[phase, z, own_slot], keep_sem.at[phase, 0]),
            pltpu.make_async_copy(o_ref.at[0], w_ref.at[phase, z, 3 + r], keep_sem.at[phase, 1]),
        )

    def deal(phase, q_ref):
        for which, j, device in ((0, 2 - 2 * core, far), (1, 1, sib)):
            slot = lax.div(3 * r + j, RANKS)
            go(
                q_ref.at[j], w_ref.at[phase, z, slot], deal_sem.at[phase, which],
                land_sem.at[phase, z, slot], device,
            )

    def along(phase, b):
        @pl.when(z < RANKS - 1)
        def _():
            line(phase, z, b, 0).start()

        @pl.when(z > 0)
        def _():
            line(phase, z, b, 1).start()

    def by_pair(zz, pair, run):
        @pl.when(lax.rem(zz + side, 2) == pair)
        def _():
            run()

    def onward(phase, zz, b):
        twin(phase, zz, b).start()
        if phase == 0 and b == 1:

            @pl.when(lax.rem(zz + side, 2) == 1)
            def _():
                out_first(phase, zz)

    def hop(phase, d, b, pair=None):
        def wanted(zz):
            return True if pair is None else lax.rem(zz + side, 2) == pair

        @pl.when((z >= d) & wanted(z + RANKS - d))
        def _():
            landed(phase, z - d, mine(phase, z - d, b))

            @pl.when(z < RANKS - 1)
            def _():
                line(phase, z - d, b, 0).start()

            onward(phase, z - d, b)

        @pl.when((z + d < RANKS) & wanted(z + d))
        def _():
            landed(phase, z + d, mine(phase, z + d, b))

            @pl.when(z > 0)
            def _():
                line(phase, z + d, b, 1).start()

            onward(phase, z + d, b)

    def from_twin(phase, zz, *which):
        for b in which:
            landed(phase, zz, theirs(phase, zz, b))


    def beside(phase, zz, which, rank):
        return block(phase, zz, 3 + rank, osib_sem.at[phase, zz, which], sib)

    def over(phase, zz):
        return block(phase, zz, 3 + r, oy_sem.at[phase, zz], far)

    def out_first(phase, zz):
        over(phase, zz).start()
        beside(phase, zz, 0, r).start()

    def out_twin(phase, zz):
        from_twin(phase, zz, 1 - phase)
        if phase == 0:
            out_first(phase, zz)
        else:
            beside(phase, zz, 0, r).start()


    def out_across(k):
        zz, rank = 2 * k + 1 - side, pair_of(r, 2)
        return block(1, zz, 3 + rank, ox_sem.at[k], other)

    def out_second(k):
        zz, rank = 2 * k + 1 - side, pair_of(r, 2)
        landed(1, zz, 3 + rank)
        out_across(k).start()
        beside(1, zz, 1, rank).start()

    def out_third(k):
        zz, rank = 2 * k + side, pair_of(r, 2)
        landed(1, zz, 3 + rank)
        beside(1, zz, 1, rank).start()

    def out_relay(phase):
        for zz in range(RANKS):
            landed(phase, zz, 3 + pair_of(r, 2))
            beside(phase, zz, 1, pair_of(r, 2)).start()

    def out_last(phase):
        for zz in range(RANKS):
            landed(phase, zz, 3 + pair_of(r, 1))
            landed(phase, zz, 3 + pair_of(r, 3))


    def normed(f, which, device):
        at = na_ref.at[f]
        return move(at, at, nsend_sem.at[which], nland_sem.at[f], device)

    def share(f, which, device):
        one = normed(f, which, device)
        one.start()
        sends.append(one)

    def project(zz, *frames):
        for f in frames:
            out = jnp.dot(
                w_ref[0, zz, 0:3].reshape(3 * head, width), na_ref[f],
                preferred_element_type=jnp.float32,
            )
            for slot in range(3):
                piece = out[slot * head : (slot + 1) * head]
                table_ref[3 * zz + slot, f, :head] = piece.astype(jnp.bfloat16)

    def project_all(zz):
        @pl.loop(0, RANKS)
        def _(f):
            project(zz, f)

    def spatial_head(i):
        @pl.loop(0, 1)
        def _(t):
            for f in range(RANKS):
                ms_ref[i, f] = attended(i, f, table_ref, head).astype(jnp.bfloat16)

        for j in (2, 3, 1):
            f = pair_of(r, j)
            go(
                ms_ref.at[i, f], mix_ref.at[RANKS * i + r], msend_sem.at[i, j],
                mland_sem.at[RANKS * i + r], {"seq": RANKS * z + f},
            )
        mix_ref[RANKS * i + r] = ms_ref[i, r]

    def mixed():
        for j in range(1, RANKS):
            for i in range(RANKS):
                h = RANKS * i + pair_of(r, j)
                move(
                    ms_ref.at[0, 0], mix_ref.at[h], msend_sem.at[0, 1], mland_sem.at[h], other
                ).wait_recv()

    def project_back(phase, lanes=slice(None)):
        @pl.loop(0, RANKS)
        def _(zz):
            update = jnp.dot(
                w_ref[phase, zz, 3:7].reshape(wide, width),
                mix_ref[:, :, lanes].reshape(width, -1),
                preferred_element_type=jnp.float32,
            )
            at = pl.ds(pl.multiple_of(zz * wide, 8), wide)
            xt_ref[at, lanes] = xt_ref[at, lanes] + update

    def normalize_again(lanes=slice(None)):
        values = xt_ref[:, lanes].astype(jnp.bfloat16).astype(jnp.float32)
        xt_ref[:, lanes] = values
        centered = values - jnp.mean(values, axis=0, keepdims=True)
        spread = jnp.mean(centered * centered, axis=0, keepdims=True)
        nb_ref[lanes, :] = (centered * lax.rsqrt(spread + epsilon)).T.astype(jnp.bfloat16)


    def rows(zz, part):
        return pl.ds(pl.multiple_of((RANKS * part + zz) * count, count), count)

    def scatter(parts=range(RANKS)):
        for part in parts:
            for j in range(1, RANKS):
                to = pair_of(z, j)
                go(
                    nb_ref.at[rows(to, part)], g_ref.at[part, RANKS * r + z],
                    asend_sem.at[part, j], gz_sem.at[part, z], {"seq": RANKS * to + r},
                )
        for part in parts:
            g_ref[part, RANKS * r + z] = nb_ref[rows(z, part), :]

    def frames(part, rank, which, device):
        at = g_ref.at[part, pl.ds(RANKS * rank, RANKS)]
        return move(at, at, fsend_sem.at[part, which], gr_sem.at[part, rank], device)

    def forward(part):
        for j in range(1, RANKS):
            source = pair_of(z, j)
            move(
                nb_ref.at[rows(0, 0)], g_ref.at[part, RANKS * r + source],
                asend_sem.at[0, 1], gz_sem.at[part, source], other,
            ).wait_recv()
        frames(part, r, 1, far).start()
        frames(part, r, 0, sib).start()

    def relay(part):
        rank = pair_of(r, 2)
        frames(part, rank, 0, sib).wait_recv()
        frames(part, rank, 2, sib).start()

    def ready(part):
        for j in (1, 3):
            frames(part, pair_of(r, j), 0, sib).wait_recv()

    def temporal(part):
        out = lax.dot_general(
            w_ref[1, :, 0:3].reshape(3 * wide, width), g_ref[part].reshape(tokens, width),
            (((1,), (1,)), ((), ())), preferred_element_type=jnp.float32,
        )
        for slot in range(3 * RANKS):
            piece = out[slot * head : (slot + 1) * head]
            table_ref[slot, part, :head] = piece.astype(jnp.bfloat16)

    def temporal_heads(part):
        @pl.loop(0, 1)
        def _(t):
            for i in range(RANKS):
                at = pl.ds(pl.multiple_of(i * head, 8), head)
                mt_ref[at, :] = attended(i, part, table_ref, head, count)

        rs_ref[part] = mt_ref[...].T.astype(jnp.bfloat16).reshape(rs_ref.shape[1:])

    def back(part, j):
        to = lax.rem(me + j, n)
        zt, rt = lax.div(to, RANKS), lax.rem(to, RANKS)
        return move(
            rs_ref.at[part, RANKS * rt + zt], mr_ref.at[r, RANKS * part + z],
            rsend_sem.at[part, j], rland_sem.at[r, RANKS * part + z], {"seq": to},
        )

    half, parts = tokens // 2, RANKS // 2

    def returned(which):
        for j in range(1, n):
            source = lax.rem(me + j, n)
            zt, rt = lax.div(source, RANKS), lax.rem(source, RANKS)
            for part in range(which * parts, (which + 1) * parts):
                move(
                    rs_ref.at[0, 0], mr_ref.at[rt, RANKS * part + zt],
                    rsend_sem.at[0, 1], rland_sem.at[rt, RANKS * part + zt], other,
                ).wait_recv()
        lanes = slice(which * half, (which + 1) * half)
        taken = slice(which * n // 2, (which + 1) * n // 2)
        for rank in range(RANKS):
            turned = mr_ref[rank, taken].reshape(half, -1).astype(jnp.float32).T
            for i in range(RANKS):
                piece = turned[i * head : (i + 1) * head]
                mix_ref[RANKS * i + rank, :, lanes] = piece.astype(jnp.bfloat16)
        project_back(1, lanes)
        out_ref[lanes, :] = xt_ref[:, lanes].T.astype(jnp.bfloat16)

    barrier = pltpu.get_barrier_semaphore()
    greeted = [other, sib, far]
    for device in greeted:
        pl.semaphore_signal(barrier, inc=1, device_id=device, device_id_type=MESH)
    for inside, way in ((z < RANKS - 1, 1), (z > 0, -1)):

        @pl.when(inside)
        def _():
            device = {"seq": me + RANKS * way}
            pl.semaphore_signal(barrier, inc=1, device_id=device, device_id_type=MESH)

    copies = [pltpu.make_async_copy(x_ref, x_vmem, keep_sem.at[2, 0])]
    copies += [*keep(0, sq_ref, so_ref), *keep(1, tq_ref, to_ref)]
    for one in copies:
        one.start()
    copies[0].wait()
    middle = (z > 0) & (z < RANKS - 1)
    pl.semaphore_wait(barrier, len(greeted) + 1 + lax.rem(lax.div(z + 1, 2), 2))

    one, two, three = (pair_of(r, j) for j in (1, 2, 3))
    near = [pair_of(z, j) for j in range(RANKS)]
    deal(0, sq_ref)
    for each in copies[1:3]:
        each.wait()
    by_pair(z, 0, lambda: along(0, 0))
    for each in copies[3:]:
        each.wait()
    by_pair(z, 1, lambda: along(1, 0))
    landed(0, z, sib_slot)
    by_pair(z, 1, lambda: along(0, 0))
    normalize_into(x_vmem, xt_ref, na_ref.at[r])
    deal(1, tq_ref)
    share(r, 1, far)
    share(r, 0, sib)
    landed(0, z, far_slot)
    by_pair(z, 0, lambda: along(0, 1))
    table_ref[2 * RANKS :, :, head:, :] = jnp.ones_like(table_ref[2 * RANKS :, :, head:, :])
    mt_ref[...] = jnp.zeros_like(mt_ref)
    hop(0, 1, 0)
    normed(one, 0, sib).wait_recv()
    project(z, r, one)
    out_first(0, z)
    hop(0, 1, 1, 0)
    hop(0, 2, 0)
    from_twin(0, near[1], 0)
    hop(0, 3, 0)
    hop(0, 2, 1, 0)
    by_pair(z, 1, lambda: along(0, 1))
    hop(0, 1, 1, 1)
    normed(two, 0, sib).wait_recv()
    share(two, 2, sib)

    @pl.when(middle)
    def _():
        hop(0, 2, 1, 1)

    landed(1, z, sib_slot)
    landed(1, z, far_slot)
    by_pair(z, 0, lambda: along(1, 0))
    along(1, 1)
    by_pair(near[1], 1, lambda: from_twin(0, near[1], 1))
    project(near[1], r, one)
    normed(three, 0, sib).wait_recv()
    project(z, two, three)
    project(near[1], two, three)
    from_twin(0, near[2], 0)
    by_pair(near[2], 1, lambda: from_twin(0, near[2], 1))
    project_all(near[2])
    hop(0, 3, 1, 0)

    @pl.when(jnp.logical_not(middle))
    def _():
        hop(0, 2, 1, 1)

    hop(0, 3, 1, 1)
    from_twin(0, near[3], 0)
    by_pair(near[3], 1, lambda: from_twin(0, near[3], 1))
    project_all(near[3])
    for j in (1, 2):
        by_pair(near[j], 0, lambda: out_twin(0, near[j]))
    hop(1, 1, 0)
    spatial_head(0)
    hop(1, 1, 1)
    spatial_head(1)
    by_pair(near[3], 0, lambda: out_twin(0, near[3]))
    hop(1, 2, 0)
    spatial_head(2)
    spatial_head(3)
    hop(1, 3, 0)
    by_pair(z, 1, lambda: out_first(1, z))
    by_pair(z, 0, lambda: beside(1, z, 0, r).start())
    for j in range(1, RANKS):
        by_pair(near[j], 1, lambda: out_first(1, near[j]))

    @pl.when(middle)
    def _():
        hop(1, 2, 1)

    out_relay(0)
    mixed()

    @pl.when(jnp.logical_not(middle))
    def _():
        hop(1, 2, 1)

    out_last(0)
    for j in range(1, RANKS):
        by_pair(near[j], 0, lambda: out_twin(1, near[j]))
    for which in range(2):
        lanes = slice(which * half, (which + 1) * half)
        project_back(0, lanes)
        normalize_again(lanes)
        scatter(range(which * parts, (which + 1) * parts))

    hop(1, 3, 1)
    for part in range(RANKS - 1):
        forward(part)
    relay(0)
    for j in range(1, RANKS):
        by_pair(near[j], 1, lambda: from_twin(1, near[j], 0))
        from_twin(1, near[j], 1)

    @pl.loop(0, RANKS)
    def _(part):
        ready(part)

        @pl.when(part == 0)
        def _():
            forward(RANKS - 1)
            for k in range(2):
                out_second(k)

        temporal(part)

        @pl.when(part < RANKS - 1)
        def _():
            relay(part + 1)

        @pl.when(part == RANKS - 1)
        def _():
            for k in range(2):
                out_third(k)

        temporal_heads(part)
        for j in range(1, n):
            back(part, j).start()
        mr_ref[r, RANKS * part + z] = rs_ref[part, RANKS * r + z]

    out_last(1)
    for which in range(2):
        returned(which)

    for one in sends:
        one.wait_send()
    for phase in range(2):
        for b in range(2):
            for zz in range(RANKS):

                @pl.when((z >= zz) & (z < RANKS - 1))
                def _():
                    line(phase, zz, b, 0).wait_send()

                @pl.when((z <= zz) & (z > 0))
                def _():
                    line(phase, zz, b, 1).wait_send()

            for j in range(1, RANKS):
                twin(phase, near[j], b).wait_send()
        for zz in range(RANKS):
            if phase == 0:
                over(phase, zz).wait_send()
            else:
                by_pair(zz, 1, lambda: over(phase, zz).wait_send())
            beside(phase, zz, 0, r).wait_send()
            beside(phase, zz, 1, two).wait_send()

    for k in range(2):
        out_across(k).wait_send()

    @pl.loop(0, RANKS)
    def _(part):
        for which, rank in ((0, r), (1, r), (2, pair_of(r, 2))):
            frames(part, rank, which, sib).wait_send()
        for j in range(1, n):
            back(part, j).wait_send()


def fused(video, spatial_qkv, spatial_out, temporal_qkv, temporal_out):
    _, tokens, width = video.shape
    n = lax.axis_size("seq")
    head, count = width // HEADS, tokens // n
    padded = -(-RANKS * head // 128) * 128
    vmem, dma = pltpu.VMEM, pltpu.SemaphoreType.DMA
    half = jnp.bfloat16

    def blocks(w):
        return w.T.reshape(-1, head, width)

    out = pl.pallas_call(
        functools.partial(fused_kernel, count),
        out_shape=jax.ShapeDtypeStruct((tokens, width), half),
        in_specs=[pl.BlockSpec(memory_space=pl.ANY)] * 5,
        out_specs=pl.BlockSpec(memory_space=pltpu.VMEM),
        scratch_shapes=[
            vmem((2, RANKS, 3 + RANKS, head, width), half),
            vmem((RANKS, width, tokens), half),
            vmem((width, tokens), jnp.float32),
            vmem((3 * RANKS, RANKS, head + 8, tokens), half),
            vmem((RANKS, RANKS, head, tokens), half),
            vmem((HEADS, head, tokens), half),
            vmem((tokens, width), half),
            vmem((RANKS, n, count, width), half),
            vmem((padded, tokens), jnp.float32),
            vmem((RANKS, n, count, padded), half),
            vmem((RANKS, n, count, padded), half),
            dma((2, RANKS, 3 + RANKS)),
            dma((2, 2)),
            dma((2, 2, RANKS, 2)),
            dma((2, RANKS, 2)),
            dma((2, RANKS, 2)),
            dma((2, RANKS)),
            dma((2,)),
            dma((RANKS,)),
            dma((3,)),
            dma((RANKS, RANKS)),
            dma((HEADS,)),
            dma((RANKS, RANKS)),
            dma((RANKS, RANKS)),
            dma((RANKS, 3)),
            dma((RANKS, RANKS)),
            dma((RANKS, n)),
            dma((RANKS, n)),
            vmem((tokens, width), half),
            dma((3, 2)),
        ],
        compiler_params=pltpu.CompilerParams(
            collective_id=0, has_side_effects=True, vmem_limit_bytes=60 << 20
        ),
    )(
        video.reshape(tokens, width),
        blocks(spatial_qkv), blocks(spatial_out), blocks(temporal_qkv), blocks(temporal_out),
    )
    return out.reshape(video.shape)


def local(video, spatial_qkv, *rest):
    n, groups = lax.axis_size("seq"), lax.axis_size("groups")
    frames_here, patches, _ = video.shape
    ringed = n == HEADS and groups % 2 == 0 and frames_here == 1 and patches % (16 * n) == 0
    return (fused if ringed else plain)(video, spatial_qkv, *rest)


def solution(mesh):
    split = P(None, "seq")
    placed = (P(("groups", "seq"), None, None), split, split, split, split)
    return jax.shard_map(
        local,
        mesh=mesh,
        in_specs=placed,
        out_specs=placed[0],
        check_vma=False,
    )
```
